512 devices in a mesh: line: 32 (over y, x, core), bus: 16 (over z).
Axes of the slice: x: 4, y: 4, z: 16, core: 2. Of those that a mesh axis runs over, the one named last changes fastest.
Arguments:
- ptdf: bfloat16 [8192, 100352], P('line', 'bus')
- base_injection: float32 [100352], P('bus'), may hold values from -6 to 6
- injection_gain: float32 [100352], P('bus'), may hold values from 0.3 to 3
- factor_of_bus: int32 [100352], P('bus'), may hold values from 0 to 511
- line_rating: int32 [8192], P('line'), may hold values from 60 to 300
- directions: int32 [30, 512], replicated, may hold values from 1 to 1073741823, as said below
- shifts: int32 [8, 512], replicated, may hold values from 0 to 1073741823
- chol_factor: float32 [512, 512], replicated
- proposal_mean: float32 [512], replicated, may hold values from -0.3 to 0.3
Outputs:
- flows: float32 [1024, 8192], P('bus', 'line')
- overload: float32 [1024], P('bus')
- weight: float32 [1024], P('bus')
- new_mean: float32 [512], replicated
The draws below stay inside these ranges and needn't reach their ends.
Inputs may be any that keep to these rules, and one draw needn't show every extreme that they name: directions[b, f] lies in [2^(29 - b), 2^(30 - b)), as Sobol direction numbers do.
All inputs are finite; a program needn't handle non-finite values.
Results may differ from the reference program's by a relative error of at most 0.0029.
Values sent between devices are 32-bit elements; how exact they have to be, the bound alone decides.
A program may use at most 64 MiB of HBM per device.

```python
import math
import jax
import jax.numpy as jnp
from jax import lax

BUS = 100352
FACTORS = 512
BITS = 30
SHIFTS = 8
POINTS = 128
SCEN = 1024
LINES = 8192


def draw_directions(key, part):
    bit_rows = jnp.arange(BITS, dtype=jnp.int32)[:, None]
    leading = jnp.left_shift(jnp.ones((BITS, FACTORS), jnp.int32), 29 - bit_rows)
    noise = jax.random.randint(key, (BITS, FACTORS), 0, 1073741824, dtype=jnp.int32)
    return leading + jnp.bitwise_and(noise, leading - 1)


def draw_chol_factor(key, part):
    entry_key = jax.random.fold_in(key, 11)
    diag_key = jax.random.fold_in(key, 12)
    entries = jax.random.normal(entry_key, (FACTORS, FACTORS), jnp.float32)
    diagonal = jnp.exp(jax.random.uniform(diag_key, (FACTORS,), jnp.float32, math.log(0.5), math.log(1.5)))
    lower = jnp.tril(entries, -1) * (0.8 / math.sqrt(FACTORS))
    return lower + jnp.eye(FACTORS, dtype=jnp.float32) * diagonal[None, :]


def draw_ptdf(key, part):
    entry_key = jax.random.fold_in(key, 21)
    row_key = jax.random.fold_in(key, 22)
    column_key = jax.random.fold_in(key, 23)
    position = jnp.arange(LINES, dtype=jnp.float32) / LINES
    entries = jax.random.normal(entry_key, (LINES, BUS), jnp.float32)
    row_spread = jnp.exp(jax.random.uniform(row_key, (LINES,), jnp.float32, math.log(0.5), math.log(2.0)))
    column_spread = jnp.exp(jax.random.uniform(column_key, (BUS,), jnp.float32, math.log(0.5), math.log(2.0)))
    row_scale = jnp.exp(math.log(3.0) * position) * row_spread
    values = entries * row_scale[:, None] * column_spread[None, :] * (0.5 / math.sqrt(BUS))
    return values.astype(jnp.bfloat16)


def set_ends(values, key, low, largest):
    longest = values.shape.index(max(values.shape))
    spots = []
    for shift in (0, 1):
        where = [jax.random.randint(jax.random.fold_in(key, axis), (), 0, length) for axis, length in enumerate(values.shape)]
        where[longest] = (where[longest] + shift) % values.shape[longest]
        spots.append(tuple(where))
    return values.at[spots[0]].set(low).at[spots[1]].set(largest)


def block_scale(rng, shape, cuts, low, top_value):
    level, own = 1.0, jax.random.fold_in(rng, 6)
    for dim, blocks in cuts:
        steps = jnp.exp(jax.random.uniform(jax.random.fold_in(own, dim), (blocks,), jnp.float32, low / len(cuts), top_value / len(cuts)))
        level = level * jnp.repeat(steps, shape[dim] // blocks).reshape([-1 if axis == dim else 1 for axis in range(len(shape))])
    return level


def bell_draw(rng, dims, scale, reach, split=(), kind=jnp.bfloat16):
    drawn = jax.random.normal(rng, dims, jnp.float32) * scale
    if len(split) > 0:
        drawn = block_scale(rng, dims, split, -0.22, 0.18) * drawn
    return jnp.clip(drawn, min=-reach, max=reach).astype(kind)


def setup_inputs(seed: int = 0) -> dict:
    arg_keys = jax.random.split(jax.random.key(seed), 10)
    return {
        "ptdf": draw_ptdf(jax.random.fold_in(arg_keys[9], 71), 0),
        "base_injection": bell_draw(arg_keys[1], (BUS,), 1.0, 6.0, ((0, 16),), jnp.float32),
        "injection_gain": jnp.clip(jnp.exp(math.log(3.0) - 2.3025851 * jax.random.uniform(arg_keys[2], (BUS,), jnp.float32) ** block_scale(arg_keys[2], (BUS,), ((0, 16),), -0.2, 0.2)), 0.3, 3.0),
        "factor_of_bus": set_ends(jax.random.randint(arg_keys[3], (BUS,), 0, FACTORS), jax.random.fold_in(arg_keys[3], 1), 0, FACTORS - 1).astype(jnp.int32),
        "line_rating": set_ends(jax.random.randint(arg_keys[4], (LINES,), 60, 301), jax.random.fold_in(arg_keys[4], 1), 60, 300).astype(jnp.int32),
        "directions": draw_directions(jax.random.fold_in(arg_keys[9], 71), 0),
        "shifts": set_ends(jax.random.randint(arg_keys[6], (SHIFTS, FACTORS), 0, 1073741824), jax.random.fold_in(arg_keys[6], 1), 0, 1073741823).astype(jnp.int32),
        "chol_factor": draw_chol_factor(jax.random.fold_in(arg_keys[9], 71), 0),
        "proposal_mean": bell_draw(arg_keys[8], (FACTORS,), 0.06, 0.3, (), jnp.float32),
    }


SHARP = 8.0

def normals(directions, shifts, start_row, row_count):
    scenario = start_row + jnp.arange(row_count, dtype=jnp.int32)
    sobol_point = scenario % POINTS
    shift_index = scenario // POINTS
    digits = jnp.zeros((row_count, directions.shape[1]), jnp.int32)
    for bit_index in range(max(1, (POINTS - 1).bit_length())):
        picked = sobol_point >> bit_index & 1
        digits = digits ^ picked[:, None] * directions[bit_index][None, :]
    chosen = (shift_index[:, None] == jnp.arange(shifts.shape[0], dtype=jnp.int32)[None, :]).astype(jnp.int32)
    offset = lax.optimization_barrier(jnp.sum(chosen[:, :, None] * shifts[None, :, :], axis=1))
    digits = digits ^ offset
    uniform = (2 * (digits >> 7) + 1).astype(jnp.float32) / 16777216.0
    return math.sqrt(2.0) * lax.erf_inv(2.0 * uniform - 1.0)

def reference(ptdf, base_injection, injection_gain, factor_of_bus, line_rating, directions, shifts, chol_factor, proposal_mean):
    high = lax.Precision.HIGHEST
    normal_draws = normals(directions, shifts, 0, SCEN)
    factors = jnp.dot(normal_draws + proposal_mean[None, :], chol_factor.T, precision=high, preferred_element_type=jnp.float32)
    picked = jnp.take(factors, factor_of_bus, axis=1)
    injections = (base_injection[None, :] + injection_gain[None, :] * picked).astype(jnp.bfloat16)
    wide_injections = injections.astype(jnp.float32)
    line_block = 512 if LINES % 512 == 0 else LINES
    blocks = ptdf.reshape(LINES // line_block, line_block, ptdf.shape[1])

    def one_block(rows):
        return jnp.dot(wide_injections, rows.astype(jnp.float32).T, precision=high, preferred_element_type=jnp.float32)
    flows = lax.map(one_block, blocks)
    flows = jnp.transpose(flows, (1, 0, 2)).reshape(SCEN, LINES)
    rating = line_rating.astype(jnp.float32) * 0.01
    overload = lax.optimization_barrier(jnp.sum(jax.nn.softplus(SHARP * (jnp.abs(flows) / rating[None, :] - 1.0)), axis=1)) / SHARP / LINES
    likelihood = jnp.exp(-jnp.dot(normal_draws, proposal_mean, precision=high, preferred_element_type=jnp.float32))
    emphasis = likelihood * overload
    total = jnp.sum(emphasis)
    weight = SCEN * likelihood * overload / total
    new_mean = proposal_mean + jnp.dot(emphasis, normal_draws, precision=high, preferred_element_type=jnp.float32) / total
    return (flows, overload, weight, new_mean)
```

```python
import functools
import math

import jax
import jax.numpy as jnp
from jax import lax
from jax.experimental import pallas as pl
from jax.experimental.pallas import tpu as pltpu
from jax.sharding import PartitionSpec as P

MESH = pl.DeviceIdType.MESH
POINTS = 128
SHARP = 8.0
F32 = jnp.float32
BF16 = jnp.bfloat16
NT = (((1,), (1,)), ((), ()))
NN = (((1,), (0,)), ((), ()))
PIECES = 2

CENTRAL = (
    2.81022636e-08,
    3.43273939e-07,
    -3.5233877e-06,
    -4.39150654e-06,
    0.00021858087,
    -0.00125372503,
    -0.00417768164,
    0.246640727,
    1.50140941,
)
TAIL = (
    -0.000200214257,
    0.000100950558,
    0.00134934322,
    -0.00367342844,
    0.00573950773,
    -0.0076224613,
    0.00943887047,
    1.00167406,
    2.83297682,
)


def dot(a, b, dims):
    return lax.dot_general(a, b, dims, preferred_element_type=F32)


def split(x):
    hi = x.astype(BF16)
    return hi, (x - hi.astype(F32)).astype(BF16)


def draw(digits):
    x = (2 * lax.shift_right_arithmetic(digits, 7) + 1).astype(F32) * (1.0 / 8388608.0) - 1.0
    w = -jnp.log((1.0 - x) * (1.0 + x))
    near = w < 5.0
    t = jnp.where(near, w - 2.5, jnp.sqrt(w) - 3.0)
    p = jnp.where(near, CENTRAL[0], TAIL[0])
    for a, b in zip(CENTRAL[1:], TAIL[1:]):
        p = jnp.where(near, a, b) + p * t
    return math.sqrt(2.0) * x * p


def kernel(
    nz,
    nl,
    ptdf_h,
    base_h,
    gain_h,
    fob_h,
    rating_h,
    dirs_h,
    shifts_h,
    chol_h,
    mean_h,
    flows_o,
    overload_o,
    weight_o,
    newmean_o,
    ptdf,
    base,
    gain,
    fob,
    rating,
    dirs,
    shifts,
    chol,
    mean,
    m_all,
    ring_p,
    ring_m,
    table,
    n_hi,
    n_lo,
    c_hi,
    c_lo,
    lik,
    base_row,
    base_in,
    send,
    recv,
    share,
    plane_in,
    plane_sum,
    deep_in,
    over,
    load_sem,
    ps,
    pr,
    ms,
    mr,
    bs,
    br,
    fs,
    fr,
    ls,
    lr,
    ds,
    dr,
):
    z = lax.axis_index("bus")
    me = lax.axis_index("line")
    lines, buses = ptdf.shape
    factors = chol.shape[0]
    half = nz // 2
    blocks = [(k, min(1024, buses - k)) for k in range(0, buses, 1024)]

    small = [
        (fob_h, fob),
        (gain_h, gain),
        (base_h, base),
        (rating_h, rating),
        (dirs_h, dirs),
        (shifts_h, shifts),
        (chol_h, chol),
        (mean_h, mean),
    ]
    loads = [pltpu.make_async_copy(a, b, load_sem.at[i]) for i, (a, b) in enumerate(small)]
    for i, (k, size) in enumerate(blocks):
        loads.append(
            pltpu.make_async_copy(
                ptdf_h.at[:, pl.ds(k, size)], ptdf.at[:, pl.ds(k, size)], load_sem.at[len(small) + i]
            )
        )
    for copy in loads:
        copy.start()

    barrier = pltpu.get_barrier_semaphore()

    def greet_z(d, carry):
        pl.semaphore_signal(
            barrier, inc=1, device_id={"bus": lax.rem(z + d, nz)}, device_id_type=MESH
        )
        return carry

    def greet_l(d, carry):
        pl.semaphore_signal(
            barrier, inc=1, device_id={"line": lax.rem(me + d, nl)}, device_id_type=MESH
        )
        return carry

    lax.fori_loop(1, nz, greet_z, 0)
    lax.fori_loop(1, nl, greet_l, 0)

    for copy in loads[: len(small)]:
        copy.wait()
    acc = jnp.zeros((lines, factors), F32)
    for i, (k, size) in enumerate(blocks):
        loads[len(small) + i].wait()
        rows = ptdf[:, pl.ds(k, size)]
        g_hi, g_lo = split(gain[:, pl.ds(k, size)])
        which = fob[:, pl.ds(k, size)]
        hit = lax.broadcasted_iota(jnp.int32, (factors, size), 0) == which
        acc += dot(rows, jnp.where(hit, g_hi.astype(F32), 0.0).astype(BF16), NT)
        acc += dot(rows, jnp.where(hit, g_lo.astype(F32), 0.0).astype(BF16), NT)
    m_all[...] = acc.reshape(m_all.shape)

    pl.semaphore_wait(barrier, nz + nl - 2)

    wide = factors // PIECES
    right = lax.rem(z + 1, nz)
    left = lax.rem(z + nz - 1, nz)

    def lanes(piece):
        return pl.ds(piece * wide, wide)

    def hop(source, ring, t, piece, send_sem, recv_sem, target):
        return pltpu.make_async_remote_copy(
            src_ref=source,
            dst_ref=ring.at[t, :, lanes(piece)],
            send_sem=send_sem.at[t, piece],
            recv_sem=recv_sem.at[t, piece],
            device_id={"bus": target},
            device_id_type=MESH,
        )

    def shadow(t):
        if t == 0:
            point = lax.broadcasted_iota(jnp.int32, (POINTS, factors), 0)
            digits = jnp.zeros((POINTS, factors), jnp.int32)
            for bit in range(7):
                picked = lax.shift_right_logical(point, bit) & 1
                digits = digits ^ (picked * dirs[bit : bit + 1, :])
            table[...] = digits
            hi, lo = split(chol[...])
            c_hi[...] = hi
            c_lo[...] = lo
        if t == 1:
            row = jnp.zeros((16, lines), F32)
            for k, size in blocks:
                hi, lo = split(base[:, pl.ds(k, size)])
                both = jnp.concatenate([hi.astype(F32), lo.astype(F32), jnp.zeros((14, size), F32)], axis=0)
                row += dot(both.astype(BF16), ptdf[:, pl.ds(k, size)], NT)
            total_row = row[0:1, :] + row[1:2, :]
            base_row[0:1, :] = total_row[:, 0 : lines // 2]
            base_row[1:2, :] = total_row[:, lines // 2 :]
        rows = pl.ds(t * POINTS, POINTS)
        normal = draw(table[...] ^ shifts[t : t + 1, :])
        hi, lo = split(normal)
        n_hi[rows, :] = hi
        n_lo[rows, :] = lo
        m_hi, m_lo = split(mean[...])
        both = jnp.concatenate(
            [m_hi.astype(F32), m_lo.astype(F32), jnp.zeros((14, factors), F32)], axis=0
        ).astype(BF16)
        first = dot(both, hi, NT)
        second = dot(both, lo, NT)
        lik[t : t + 1, :] = jnp.exp(-(first[0:1, :] + (first[1:2, :] + second[0:1, :])))

    sent = []
    for t in range(half):
        for piece in range(PIECES):
            if t == 0:
                source = m_all.at[lax.rem(z + half, nz), :, lanes(piece)]
            else:
                sent_in = hop(ring_p.at[t - 1, :, lanes(piece)], ring_p, t - 1, piece, ps, pr, right)
                sent_in.wait_recv()
                ring_p[t - 1, :, lanes(piece)] += m_all[lax.rem(z + half - t, nz), :, lanes(piece)]
                source = ring_p.at[t - 1, :, lanes(piece)]
            copy = hop(source, ring_p, t, piece, ps, pr, right)
            copy.start()
            sent.append(copy)
            if t == half - 1:
                continue
            if t == 0:
                source = m_all.at[lax.rem(z + nz - half + 1, nz), :, lanes(piece)]
            else:
                sent_in = hop(ring_m.at[t - 1, :, lanes(piece)], ring_m, t - 1, piece, ms, mr, left)
                sent_in.wait_recv()
                ring_m[t - 1, :, lanes(piece)] += m_all[
                    lax.rem(z + nz - half + 1 + t, nz), :, lanes(piece)
                ]
                source = ring_m.at[t - 1, :, lanes(piece)]
            copy = hop(source, ring_m, t, piece, ms, mr, left)
            copy.start()
            sent.append(copy)
        shadow(t)
        if t == 1:
            for d in range(1, nz):
                peer = lax.rem(z + d, nz)
                copy = pltpu.make_async_remote_copy(
                    src_ref=base_row,
                    dst_ref=base_in.at[z],
                    send_sem=bs.at[d],
                    recv_sem=br.at[z],
                    device_id={"bus": peer},
                    device_id_type=MESH,
                )
                copy.start()
                sent.append(copy)
            base_in[z] = base_row[...]

    for d in range(1, nz):
        peer = lax.rem(z + d, nz)
        pltpu.make_async_remote_copy(
            src_ref=base_row,
            dst_ref=base_in.at[peer],
            send_sem=bs.at[d],
            recv_sem=br.at[peer],
            device_id={"bus": peer},
            device_id_type=MESH,
        ).wait_recv()
    own_lines = lines // nz
    base_sum = base_in[0]
    for j in range(1, nz):
        base_sum = base_sum + base_in[j]
    base_line = jnp.concatenate([base_sum[0:1, :], base_sum[1:2, :]], axis=1)
    mine = lax.broadcasted_iota(jnp.int32, (own_lines, lines), 1) == (
        lax.broadcasted_iota(jnp.int32, (own_lines, lines), 0) + z * own_lines
    )
    base_col = jnp.sum(jnp.where(mine, base_line, 0.0), axis=1, keepdims=True)
    rate_col = jnp.sum(jnp.where(mine, rating[...].astype(F32) * 0.01, 0.0), axis=1, keepdims=True)
    steep = SHARP / rate_col

    total_m = m_all[z]
    parts = []
    for piece in range(PIECES):
        hop(ring_p.at[half - 1, :, lanes(piece)], ring_p, half - 1, piece, ps, pr, right).wait_recv()
        hop(ring_m.at[half - 2, :, lanes(piece)], ring_m, half - 2, piece, ms, mr, left).wait_recv()
    total_m = total_m + ring_p[half - 1] + ring_m[half - 2]

    h, l = split(total_m)
    g = dot(h, c_hi[...], NN) + (dot(l, c_hi[...], NN) + dot(h, c_lo[...], NN))
    const = jnp.sum(g * mean[...], axis=1, keepdims=True) + base_col
    gh, gl = split(g)
    both = jnp.concatenate([gh.astype(F32), gl.astype(F32)], axis=0).astype(BF16)
    low_lane = lax.broadcasted_iota(jnp.int32, (8, POINTS), 1) < POINTS // 2
    for k in range(8):
        rows = pl.ds(k * POINTS, POINTS)
        first = dot(both, n_hi[rows, :], NT)
        second = dot(gh, n_lo[rows, :], NT)
        x = first[0:own_lines, :] + (first[own_lines:, :] + second) + const
        v = jnp.abs(x) * steep - SHARP
        soft = jnp.maximum(v, 0.0) + jnp.log1p(jnp.exp(-jnp.abs(v)))
        share[k : k + 1, :] = jnp.sum(soft, axis=0, keepdims=True) * (1.0 / (SHARP * lines * nl))
        top, low = x[0:8, :], x[8:16, :]
        send[2 * k] = jnp.where(low_lane, top, pltpu.roll(low, POINTS // 2, 1))
        send[2 * k + 1] = jnp.where(low_lane, pltpu.roll(top, POINTS // 2, 1), low)

    def plane_copy(peer, slot, d):
        return pltpu.make_async_remote_copy(
            src_ref=share,
            dst_ref=plane_in.at[slot],
            send_sem=ls.at[d],
            recv_sem=lr.at[slot],
            device_id={"line": peer},
            device_id_type=MESH,
        )

    def plane_start(d, carry):
        plane_copy(lax.rem(me + d, nl), me, d).start()
        return carry

    def plane_wait(d, carry):
        peer = lax.rem(me + d, nl)
        plane_copy(peer, peer, d).wait()
        return carry

    def flow_copy(peer, slot, d):
        return pltpu.make_async_remote_copy(
            src_ref=send.at[peer],
            dst_ref=recv.at[slot],
            send_sem=fs.at[d],
            recv_sem=fr.at[slot],
            device_id={"bus": peer},
            device_id_type=MESH,
        )

    def flow_start(d, carry):
        flow_copy(lax.rem(z + d, nz), z, d).start()
        return carry

    def flow_wait(d, carry):
        peer = lax.rem(z + d, nz)
        flow_copy(peer, peer, d).wait()
        return carry

    def deep_copy(peer, slot, d):
        return pltpu.make_async_remote_copy(
            src_ref=plane_sum,
            dst_ref=deep_in.at[slot],
            send_sem=ds.at[d],
            recv_sem=dr.at[slot],
            device_id={"bus": peer},
            device_id_type=MESH,
        )

    def deep_start(d, carry):
        deep_copy(lax.rem(z + d, nz), z, d).start()
        return carry

    def deep_wait(d, carry):
        peer = lax.rem(z + d, nz)
        deep_copy(peer, peer, d).wait()
        return carry

    lax.fori_loop(1, nl, plane_start, 0)
    lax.fori_loop(1, nz, flow_start, 0)
    plane_in[me] = share[...]
    recv[z] = send[z]
    lax.fori_loop(1, nl, plane_wait, 0)
    partial = plane_in[0]
    for j in range(1, nl):
        partial = partial + plane_in[j]
    plane_sum[...] = partial
    lax.fori_loop(1, nz, deep_start, 0)
    deep_in[z] = partial

    lax.fori_loop(1, nz, flow_wait, 0)
    tiles = []
    for j in range(nz):
        tile = recv[j]
        tiles.append(tile)
        tiles.append(pltpu.roll(tile, POINTS // 2, 1))
    by_line = jnp.concatenate(tiles, axis=0)
    flows_o[...] = jnp.transpose(by_line)[0 : POINTS // 2, :]

    lax.fori_loop(1, nz, deep_wait, 0)
    total_over = deep_in[0]
    for j in range(1, nz):
        total_over = total_over + deep_in[j]
    over[...] = total_over
    emphasis = lik[...] * total_over
    total = jnp.sum(jnp.sum(emphasis, axis=1, keepdims=True), axis=0, keepdims=True)
    inverse = 1.0 / total
    flat = jnp.concatenate([emphasis[k : k + 1, :] for k in range(8)], axis=1)
    e_hi, e_lo = split(flat)
    both = jnp.concatenate(
        [e_hi.astype(F32), e_lo.astype(F32), jnp.zeros((14, flat.shape[1]), F32)], axis=0
    ).astype(BF16)
    first = dot(both, n_hi[...], NN)
    second = dot(both, n_lo[...], NN)
    moved = first[0:1, :] + (first[1:2, :] + second[0:1, :])
    newmean_o[...] = mean[...] + moved * inverse
    row = over[pl.ds(z // 2, 1), :]
    like_row = lik[pl.ds(z // 2, 1), :]
    odd = lax.rem(z, 2) == 1
    row = jnp.where(odd, row[:, POINTS // 2 :], row[:, 0 : POINTS // 2])
    like_row = jnp.where(odd, like_row[:, POINTS // 2 :], like_row[:, 0 : POINTS // 2])
    overload_o[...] = row
    weight_o[...] = (float(8 * POINTS) * like_row) * row * inverse

    for copy in sent:
        copy.wait_send()


def per_device(nz, nl, ptdf, base, gain, fob, rating, dirs, shifts, chol, mean):
    lines, buses = ptdf.shape
    factors = chol.shape[0]
    half = nz // 2
    own = lines // nz
    scen = shifts.shape[0] * POINTS
    vm, dma = pltpu.VMEM, pltpu.SemaphoreType.DMA
    anywhere = pl.BlockSpec(memory_space=pl.ANY)
    inside = pl.BlockSpec(memory_space=pltpu.VMEM)
    n_loads = 8 + -(-buses // 1024)
    flows, overload, weight, new_mean = pl.pallas_call(
        functools.partial(kernel, nz, nl),
        out_shape=(
            jax.ShapeDtypeStruct((scen // nz, lines), F32),
            jax.ShapeDtypeStruct((1, scen // nz), F32),
            jax.ShapeDtypeStruct((1, scen // nz), F32),
            jax.ShapeDtypeStruct((1, factors), F32),
        ),
        in_specs=[anywhere] * 9,
        out_specs=(inside,) * 4,
        scratch_shapes=[
            vm((lines, buses), BF16),
            vm((1, buses), F32),
            vm((1, buses), F32),
            vm((1, buses), jnp.int32),
            vm((1, lines), jnp.int32),
            vm(dirs.shape, jnp.int32),
            vm(shifts.shape, jnp.int32),
            vm(chol.shape, F32),
            vm((1, factors), F32),
            vm((nz, own, factors), F32),
            vm((half, own, factors), F32),
            vm((half - 1, own, factors), F32),
            vm((POINTS, factors), jnp.int32),
            vm((scen, factors), BF16),
            vm((scen, factors), BF16),
            vm(chol.shape, BF16),
            vm(chol.shape, BF16),
            vm((8, POINTS), F32),
            vm((2, POINTS), F32),
            vm((nz, 2, POINTS), F32),
            vm((nz, 8, POINTS), F32),
            vm((nz, 8, POINTS), F32),
            vm((8, POINTS), F32),
            vm((nl, 8, POINTS), F32),
            vm((8, POINTS), F32),
            vm((nz, 8, POINTS), F32),
            vm((8, POINTS), F32),
            dma((n_loads,)),
            dma((half, PIECES)),
            dma((half, PIECES)),
            dma((half - 1, PIECES)),
            dma((half - 1, PIECES)),
            dma((nz,)),
            dma((nz,)),
            dma((nz,)),
            dma((nz,)),
            dma((nl,)),
            dma((nl,)),
            dma((nz,)),
            dma((nz,)),
        ],
        compiler_params=pltpu.CompilerParams(
            collective_id=0, has_side_effects=True, vmem_limit_bytes=40 * 1024 * 1024
        ),
    )(
        ptdf,
        base.reshape(1, buses),
        gain.reshape(1, buses),
        fob.reshape(1, buses),
        rating.reshape(1, lines),
        dirs,
        shifts,
        chol,
        mean.reshape(1, factors),
    )
    return flows, overload.reshape(-1), weight.reshape(-1), new_mean.reshape(-1)


def solution(mesh):
    nz, nl = mesh.shape["bus"], mesh.shape["line"]
    return jax.shard_map(
        functools.partial(per_device, nz, nl),
        mesh=mesh,
        in_specs=(P("line", "bus"), P("bus"), P("bus"), P("bus"), P("line"), P(), P(), P(), P()),
        out_specs=(P("bus", "line"), P("bus"), P("bus"), P()),
        check_vma=False,
    )
```

```python
import functools
import math

import jax
import jax.numpy as jnp
from jax import lax
from jax.experimental import pallas as pl
from jax.experimental.pallas import tpu as pltpu
from jax.sharding import PartitionSpec as P

MESH = pl.DeviceIdType.MESH
POINTS = 128
SHARP = 8.0
F32 = jnp.float32
BF16 = jnp.bfloat16
NT = (((1,), (1,)), ((), ()))
NN = (((1,), (0,)), ((), ()))
PIECES = 2
PLUS = (6, 3, 0)
MINUS = (5, 2, 0)
GAPS = ((0, 1, 2), (3, 4, 5), (6, 7))

CENTRAL = (
    2.81022636e-08,
    3.43273939e-07,
    -3.5233877e-06,
    -4.39150654e-06,
    0.00021858087,
    -0.00125372503,
    -0.00417768164,
    0.246640727,
    1.50140941,
)
TAIL = (
    -0.000200214257,
    0.000100950558,
    0.00134934322,
    -0.00367342844,
    0.00573950773,
    -0.0076224613,
    0.00943887047,
    1.00167406,
    2.83297682,
)


def dot(a, b, dims):
    return lax.dot_general(a, b, dims, preferred_element_type=F32)


def split(x):
    hi = x.astype(BF16)
    return hi, (x - hi.astype(F32)).astype(BF16)


def draw(digits):
    x = (2 * lax.shift_right_arithmetic(digits, 7) + 1).astype(F32) * (1.0 / 8388608.0) - 1.0
    w = -jnp.log((1.0 - x) * (1.0 + x))
    near = w < 5.0
    t = jnp.where(near, w - 2.5, jnp.sqrt(w) - 3.0)
    p = jnp.where(near, CENTRAL[0], TAIL[0])
    for a, b in zip(CENTRAL[1:], TAIL[1:]):
        p = jnp.where(near, a, b) + p * t
    return math.sqrt(2.0) * x * p


def next_stop(stops, k):
    return max(c for c in stops if c < k)


def far_first(offsets, sizes):
    reach = [sum(min(o, n - o) for o, n in zip(off, sizes)) for off in offsets]
    return [offsets[i] for i in sorted(range(len(offsets)), key=lambda i: -reach[i])]


def kernel(
    nz,
    nl,
    ptdf_h,
    base_h,
    gain_h,
    fob_h,
    rating_h,
    dirs_h,
    shifts_h,
    chol_h,
    mean_h,
    flows_o,
    overload_o,
    weight_o,
    newmean_o,
    ptdf,
    base,
    gain,
    fob,
    rating,
    dirs,
    shifts,
    chol,
    mean,
    m_all,
    ring_p,
    ring_m,
    table,
    n_hi,
    n_lo,
    c_hi,
    c_lo,
    lik,
    base_row,
    base_in,
    send,
    recv,
    share,
    pair_in,
    chip_sum,
    plane_in,
    plane_sum,
    deep_in,
    over,
    load_sem,
    ps,
    pr,
    ms,
    mr,
    bs,
    br,
    fs,
    fr,
    cs,
    cr,
    ls,
    lr,
    ds,
    dr,
):
    z = lax.axis_index("bus")
    me = lax.axis_index("line")
    lines, buses = ptdf.shape
    factors = chol.shape[0]
    half = nz // 2
    cut = buses // 2 // 128 * 128 + 128
    blocks = [(0, cut), (cut, buses - cut)]
    chip, core = me // 2, lax.rem(me, 2)
    row_of, col_of = chip // 4, lax.rem(chip, 4)
    z_order = [d for (d,) in far_first([(d,) for d in range(1, nz)], (nz,))]
    plane_order = far_first([(i, j) for i in range(4) for j in range(4) if i + j > 0], (4, 4))

    def chip_at(i, j):
        return lax.rem(row_of + i, 4) * 4 + lax.rem(col_of + j, 4)

    first = [(fob_h, fob), (gain_h, gain), (base_h, base)]
    later = [
        (rating_h, rating),
        (dirs_h, dirs),
        (shifts_h, shifts),
        (chol_h, chol),
        (mean_h, mean),
    ]
    pairs = list(first)
    for k, size in blocks:
        pairs.append((ptdf_h.at[:, pl.ds(k, size)], ptdf.at[:, pl.ds(k, size)]))
    pairs += later
    loads = [pltpu.make_async_copy(a, b, load_sem.at[i]) for i, (a, b) in enumerate(pairs)]
    for copy in loads:
        copy.start()

    barrier = pltpu.get_barrier_semaphore()

    def greet_z(d, carry):
        pl.semaphore_signal(
            barrier, inc=1, device_id={"bus": lax.rem(z + d, nz)}, device_id_type=MESH
        )
        return carry

    lax.fori_loop(1, nz, greet_z, 0)
    for i, j in plane_order:
        pl.semaphore_signal(
            barrier,
            inc=1,
            device_id={"line": chip_at(i, j) * 2 + core},
            device_id_type=MESH,
        )
    pl.semaphore_signal(
        barrier, inc=1, device_id={"line": chip * 2 + 1 - core}, device_id_type=MESH
    )

    wide = factors // PIECES

    factor = lax.broadcasted_iota(jnp.int32, (wide, 128), 0).astype(F32).astype(BF16)
    nothing = jnp.zeros((wide, 128), BF16)

    def gather(piece):
        acc = None
        for i, (k, size) in enumerate(blocks):
            if piece == 0:
                loads[len(first) + i].wait()
            g_hi, g_lo = split(gain[pl.ds(k, size)].reshape(1, size))
            which = (fob[pl.ds(k, size)].reshape(1, size) - wide * piece).astype(F32).astype(BF16)
            hi, lo = [], []
            for j in range(0, size, 128):
                hit = factor == jnp.broadcast_to(which[:, j : j + 128], (wide, 128))
                hi.append(jnp.where(hit, jnp.broadcast_to(g_hi[:, j : j + 128], (wide, 128)), nothing))
                lo.append(jnp.where(hit, jnp.broadcast_to(g_lo[:, j : j + 128], (wide, 128)), nothing))
            stack = [jnp.concatenate(hi, axis=1), jnp.concatenate(lo, axis=1)]
            if piece == 0:
                b_hi, b_lo = split(base[pl.ds(k, size)].reshape(1, size))
                stack.append(
                    jnp.concatenate(
                        [b_hi.astype(F32), b_lo.astype(F32), jnp.zeros((14, size), F32)], axis=0
                    ).astype(BF16)
                )
            part = dot(jnp.concatenate(stack, axis=0), ptdf[:, pl.ds(k, size)], NT)
            acc = part if acc is None else acc + part
        by_line = jnp.transpose(acc[0:wide] + acc[wide : 2 * wide])
        m_all[:, :, wide * piece : wide * (piece + 1)] = by_line.reshape(nz, lines // nz, wide)
        if piece == 0:
            total_row = acc[2 * wide : 2 * wide + 1] + acc[2 * wide + 1 : 2 * wide + 2]
            base_row[0:1, :] = total_row[:, 0 : lines // 2]
            base_row[1:2, :] = total_row[:, lines // 2 :]

    def lanes(piece):
        return pl.ds(piece * wide, wide)

    sides = (
        (1, PLUS, half, ring_p, ps, pr),
        (-1, MINUS, half - 1, ring_m, ms, mr),
    )

    def toward(sign, k):
        return lax.rem(z + sign * k + nz, nz)

    def hop(side, k, piece, source):
        sign, stops, far, ring, send_sem, recv_sem = side
        return pltpu.make_async_remote_copy(
            src_ref=source,
            dst_ref=ring.at[k, :, lanes(piece)],
            send_sem=send_sem.at[k, piece],
            recv_sem=recv_sem.at[k, piece],
            device_id={"bus": toward(sign, k - next_stop(stops, k))},
            device_id_type=MESH,
        )

    def arrived(side, k, piece):
        hop(side, k, piece, side[3].at[k, :, lanes(piece)]).wait_recv()

    sent = []

    def direct(piece):
        far = max(side[2] for side in sides)
        for k in range(far, 0, -1):
            for side in sides:
                if k <= side[2] and k not in side[1]:
                    copy = hop(side, k, piece, m_all.at[toward(side[0], k), :, lanes(piece)])
                    copy.start()
                    sent.append(copy)

    def merge(level, piece):
        for side in sides:
            sign, stops, far, ring, _, _ = side
            if level >= len(stops) - 1:
                continue
            c = stops[level]
            members = [k for k in range(far, 0, -1) if next_stop(stops, k) == c]
            block = m_all[toward(sign, c), :, lanes(piece)]
            for k in members:
                arrived(side, k, piece)
                block = block + ring[k, :, lanes(piece)]
            ring[members[0], :, lanes(piece)] = block
            copy = hop(side, c, piece, ring.at[members[0], :, lanes(piece)])
            copy.start()
            sent.append(copy)

    def prepare():
        for copy in loads[len(first) + len(blocks) :]:
            copy.wait()
        point = lax.broadcasted_iota(jnp.int32, (POINTS, factors), 0)
        digits = jnp.zeros((POINTS, factors), jnp.int32)
        for bit in range(7):
            picked = lax.shift_right_logical(point, bit) & 1
            digits = digits ^ (picked * dirs[bit : bit + 1, :])
        table[...] = digits
        hi, lo = split(chol[...])
        c_hi[...] = hi
        c_lo[...] = lo

    def shadow(t):
        rows = pl.ds(t * POINTS, POINTS)
        normal = draw(table[...] ^ shifts[t : t + 1, :])
        hi, lo = split(normal)
        n_hi[rows, :] = hi
        n_lo[rows, :] = lo
        m_hi, m_lo = split(mean[...].reshape(1, factors))
        both = jnp.concatenate(
            [m_hi.astype(F32), m_lo.astype(F32), jnp.zeros((14, factors), F32)], axis=0
        ).astype(BF16)
        first = dot(both, hi, NT)
        second = dot(both, lo, NT)
        lik[t : t + 1, :] = jnp.exp(-(first[0:1, :] + (first[1:2, :] + second[0:1, :])))

    def base_copy(d, slot):
        return pltpu.make_async_remote_copy(
            src_ref=base_row,
            dst_ref=base_in.at[slot],
            send_sem=bs.at[d],
            recv_sem=br.at[slot],
            device_id={"bus": lax.rem(z + d, nz)},
            device_id_type=MESH,
        )

    for copy in loads[: len(first)]:
        copy.wait()
    gather(0)
    pl.semaphore_wait(barrier, nz + nl // 2 - 1)
    direct(0)
    for d in z_order:
        copy = base_copy(d, z)
        copy.start()
        sent.append(copy)
    base_in[z] = base_row[...]
    for piece in range(1, PIECES):
        gather(piece)
        direct(piece)
    prepare()
    for level in range(len(PLUS)):
        for t in GAPS[level]:
            shadow(t)
        if level < len(PLUS) - 1:
            for piece in range(PIECES):
                merge(level, piece)

    for d in z_order:
        base_copy(d, lax.rem(z + d, nz)).wait_recv()
    own_lines = lines // nz
    base_sum = base_in[0]
    for j in range(1, nz):
        base_sum = base_sum + base_in[j]
    base_line = jnp.concatenate([base_sum[0:1, :], base_sum[1:2, :]], axis=1)
    mine = lax.broadcasted_iota(jnp.int32, (own_lines, lines), 1) == (
        lax.broadcasted_iota(jnp.int32, (own_lines, lines), 0) + z * own_lines
    )
    base_col = jnp.sum(jnp.where(mine, base_line, 0.0), axis=1, keepdims=True)
    rate_col = jnp.sum(jnp.where(mine, rating[...].reshape(1, lines).astype(F32) * 0.01, 0.0), axis=1, keepdims=True)
    steep = SHARP / rate_col

    total_m = m_all[z]
    for side in sides:
        for k in range(side[2], 0, -1):
            if next_stop(side[1], k) == 0:
                for piece in range(PIECES):
                    arrived(side, k, piece)
                total_m = total_m + side[3][k]

    h, l = split(total_m)
    g = dot(h, c_hi[...], NN) + (dot(l, c_hi[...], NN) + dot(h, c_lo[...], NN))
    const = jnp.sum(g * mean[...].reshape(1, factors), axis=1, keepdims=True) + base_col
    gh, gl = split(g)
    both = jnp.concatenate([gh.astype(F32), gl.astype(F32)], axis=0).astype(BF16)
    low_lane = lax.broadcasted_iota(jnp.int32, (8, POINTS), 1) < POINTS // 2
    for k in range(8):
        rows = pl.ds(k * POINTS, POINTS)
        first = dot(both, n_hi[rows, :], NT)
        second = dot(gh, n_lo[rows, :], NT)
        x = first[0:own_lines, :] + (first[own_lines:, :] + second) + const
        v = jnp.abs(x) * steep - SHARP
        soft = jnp.maximum(v, 0.0) + jnp.log1p(jnp.exp(-jnp.abs(v)))
        share[k : k + 1, :] = jnp.sum(soft, axis=0, keepdims=True) * (1.0 / (SHARP * lines * nl))
        top, low = x[0:8, :], x[8:16, :]
        send[2 * k] = jnp.where(low_lane, top, pltpu.roll(low, POINTS // 2, 1))
        send[2 * k + 1] = jnp.where(low_lane, pltpu.roll(top, POINTS // 2, 1), low)

    def send_to(source, slots, slot, send_sem, recv_sem, axis, peer):
        return pltpu.make_async_remote_copy(
            src_ref=source,
            dst_ref=slots.at[slot],
            send_sem=send_sem,
            recv_sem=recv_sem,
            device_id={axis: peer},
            device_id_type=MESH,
        )

    partner = pltpu.make_async_remote_copy(
        src_ref=share,
        dst_ref=pair_in,
        send_sem=cs,
        recv_sem=cr,
        device_id={"line": chip * 2 + 1 - core},
        device_id_type=MESH,
    )
    partner.start()
    recv[z] = send[z]
    partner.wait_recv()
    chip_sum[...] = share[...] + pair_in[...]

    def plane_copy(n, slot):
        peer = chip_at(*plane_order[n])
        slot = chip if slot is None else peer
        return send_to(chip_sum, plane_in, slot, ls.at[n], lr.at[slot], "line", peer * 2 + core)

    def flow_copy(d, slot):
        peer = lax.rem(z + d, nz)
        slot = z if slot is None else peer
        return send_to(send.at[peer], recv, slot, fs.at[d], fr.at[slot], "bus", peer)

    def deep_copy(d, slot):
        peer = lax.rem(z + d, nz)
        slot = z if slot is None else peer
        return send_to(plane_sum, deep_in, slot, ds.at[d], dr.at[slot], "bus", peer)

    for n in range(len(plane_order)):
        copy = plane_copy(n, None)
        copy.start()
        sent.append(copy)
    for d in z_order:
        copy = flow_copy(d, None)
        copy.start()
        sent.append(copy)
    plane_in[chip] = chip_sum[...]
    for n in range(len(plane_order)):
        plane_copy(n, n).wait_recv()
    partial = plane_in[0]
    for j in range(1, nl // 2):
        partial = partial + plane_in[j]
    plane_sum[...] = partial
    for d in z_order:
        copy = deep_copy(d, None)
        copy.start()
        sent.append(copy)
    deep_in[z] = partial

    for d in z_order:
        flow_copy(d, d).wait_recv()
    tiles = []
    for j in range(nz):
        tile = recv[j]
        tiles.append(tile)
        tiles.append(pltpu.roll(tile, POINTS // 2, 1))
    by_line = jnp.concatenate(tiles, axis=0)
    flows_o[...] = jnp.transpose(by_line)[0 : POINTS // 2, :]

    for d in z_order:
        deep_copy(d, d).wait_recv()
    total_over = deep_in[0]
    for j in range(1, nz):
        total_over = total_over + deep_in[j]
    over[...] = total_over
    emphasis = lik[...] * total_over
    total = jnp.sum(jnp.sum(emphasis, axis=1, keepdims=True), axis=0, keepdims=True)
    inverse = 1.0 / total
    flat = jnp.concatenate([emphasis[k : k + 1, :] for k in range(8)], axis=1)
    e_hi, e_lo = split(flat)
    both = jnp.concatenate(
        [e_hi.astype(F32), e_lo.astype(F32), jnp.zeros((14, flat.shape[1]), F32)], axis=0
    ).astype(BF16)
    first = dot(both, n_hi[...], NN)
    second = dot(both, n_lo[...], NN)
    moved = first[0:1, :] + (first[1:2, :] + second[0:1, :])
    newmean_o[...] = mean[...].reshape(1, factors) + moved * inverse
    row = over[pl.ds(z // 2, 1), :]
    like_row = lik[pl.ds(z // 2, 1), :]
    odd = lax.rem(z, 2) == 1
    row = jnp.where(odd, row[:, POINTS // 2 :], row[:, 0 : POINTS // 2])
    like_row = jnp.where(odd, like_row[:, POINTS // 2 :], like_row[:, 0 : POINTS // 2])
    overload_o[...] = row
    weight_o[...] = (float(8 * POINTS) * like_row) * row * inverse

    partner.wait_send()
    for copy in sent:
        copy.wait_send()


def per_device(nz, nl, ptdf, base, gain, fob, rating, dirs, shifts, chol, mean):
    lines, buses = ptdf.shape
    factors = chol.shape[0]
    half = nz // 2
    own = lines // nz
    scen = shifts.shape[0] * POINTS
    vm, dma = pltpu.VMEM, pltpu.SemaphoreType.DMA
    anywhere = pl.BlockSpec(memory_space=pl.ANY)
    inside = pl.BlockSpec(memory_space=pltpu.VMEM)
    n_loads = 10
    flows, overload, weight, new_mean = pl.pallas_call(
        functools.partial(kernel, nz, nl),
        out_shape=(
            jax.ShapeDtypeStruct((scen // nz, lines), F32),
            jax.ShapeDtypeStruct((1, scen // nz), F32),
            jax.ShapeDtypeStruct((1, scen // nz), F32),
            jax.ShapeDtypeStruct((1, factors), F32),
        ),
        in_specs=[anywhere] * 9,
        out_specs=(inside,) * 4,
        scratch_shapes=[
            vm((lines, buses), BF16),
            vm((buses,), F32),
            vm((buses,), F32),
            vm((buses,), jnp.int32),
            vm((lines,), jnp.int32),
            vm(dirs.shape, jnp.int32),
            vm(shifts.shape, jnp.int32),
            vm(chol.shape, F32),
            vm((factors,), F32),
            vm((nz, own, factors), F32),
            vm((half + 1, own, factors), F32),
            vm((half, own, factors), F32),
            vm((POINTS, factors), jnp.int32),
            vm((scen, factors), BF16),
            vm((scen, factors), BF16),
            vm(chol.shape, BF16),
            vm(chol.shape, BF16),
            vm((8, POINTS), F32),
            vm((2, POINTS), F32),
            vm((nz, 2, POINTS), F32),
            vm((nz, 8, POINTS), F32),
            vm((nz, 8, POINTS), F32),
            vm((8, POINTS), F32),
            vm((8, POINTS), F32),
            vm((8, POINTS), F32),
            vm((nl // 2, 8, POINTS), F32),
            vm((8, POINTS), F32),
            vm((nz, 8, POINTS), F32),
            vm((8, POINTS), F32),
            dma((n_loads,)),
            dma((half + 1, PIECES)),
            dma((half + 1, PIECES)),
            dma((half, PIECES)),
            dma((half, PIECES)),
            dma((nz,)),
            dma((nz,)),
            dma((nz,)),
            dma((nz,)),
            dma(()),
            dma(()),
            dma((nl // 2,)),
            dma((nl // 2,)),
            dma((nz,)),
            dma((nz,)),
        ],
        compiler_params=pltpu.CompilerParams(
            collective_id=0, has_side_effects=True, vmem_limit_bytes=40 * 1024 * 1024
        ),
    )(
        *[
            pltpu.with_memory_space_constraint(a, pltpu.HBM)
            for a in (ptdf, base, gain, fob, rating, dirs, shifts, chol, mean)
        ]
    )
    return flows, overload.reshape(-1), weight.reshape(-1), new_mean.reshape(-1)


def solution(mesh):
    nz, nl = mesh.shape["bus"], mesh.shape["line"]
    return jax.shard_map(
        functools.partial(per_device, nz, nl),
        mesh=mesh,
        in_specs=(P("line", "bus"), P("bus"), P("bus"), P("bus"), P("line"), P(), P(), P(), P()),
        out_specs=(P("bus", "line"), P("bus"), P("bus"), P()),
        check_vma=False,
    )
```

```python
import functools
import math

import jax
import jax.numpy as jnp
from jax import lax
from jax.experimental import pallas as pl
from jax.experimental.pallas import tpu as pltpu
from jax.sharding import PartitionSpec as P

MESH = pl.DeviceIdType.MESH
POINTS = 128
SHARP = 8.0
F32 = jnp.float32
BF16 = jnp.bfloat16
NT = (((1,), (1,)), ((), ()))
NN = (((1,), (0,)), ((), ()))
WIDTHS = (256, 256)
PIECES = len(WIDTHS)
LONG = (6, 3, 0)
SHORT = (5, 2, 0)
GAPS = ((0, 1), (2, 3, 4), (5, 6, 7))

CENTRAL = (
    2.81022636e-08,
    3.43273939e-07,
    -3.5233877e-06,
    -4.39150654e-06,
    0.00021858087,
    -0.00125372503,
    -0.00417768164,
    0.246640727,
    1.50140941,
)
TAIL = (
    -0.000200214257,
    0.000100950558,
    0.00134934322,
    -0.00367342844,
    0.00573950773,
    -0.0076224613,
    0.00943887047,
    1.00167406,
    2.83297682,
)


def dot(a, b, dims):
    return lax.dot_general(a, b, dims, preferred_element_type=F32)


def split(x):
    hi = x.astype(BF16)
    return hi, (x - hi.astype(F32)).astype(BF16)


def draw(digits):
    x = (2 * lax.shift_right_arithmetic(digits, 7) + 1).astype(F32) * (1.0 / 8388608.0) - 1.0
    w = -jnp.log((1.0 - x) * (1.0 + x))
    near = w < 5.0
    t = jnp.where(near, w - 2.5, jnp.sqrt(w) - 3.0)
    p = jnp.where(near, CENTRAL[0], TAIL[0])
    for a, b in zip(CENTRAL[1:], TAIL[1:]):
        p = jnp.where(near, a, b) + p * t
    return math.sqrt(2.0) * x * p


def next_stop(stops, k):
    return max(c for c in stops if c < k)


def far_first(offsets, sizes):
    reach = [sum(min(o, n - o) for o, n in zip(off, sizes)) for off in offsets]
    return [offsets[i] for i in sorted(range(len(offsets)), key=lambda i: -reach[i])]


def kernel(
    nz,
    nl,
    ptdf_h,
    base_h,
    gain_h,
    fob_h,
    rating_h,
    dirs_h,
    shifts_h,
    chol_h,
    mean_h,
    flows_o,
    overload_o,
    weight_o,
    newmean_o,
    ptdf,
    base,
    gain,
    fob,
    rating,
    dirs,
    shifts,
    chol,
    mean,
    m_all,
    ring,
    table,
    n_hi,
    n_lo,
    c_hi,
    c_lo,
    lik,
    base_row,
    base_in,
    send,
    recv,
    share,
    pair_in,
    chip_sum,
    plane_in,
    plane_sum,
    deep_in,
    over,
    load_sem,
    ring_s,
    ring_r,
    fs,
    fr,
    cs,
    cr,
    ls,
    lr,
    ds,
    dr,
):
    z = lax.axis_index("bus")
    me = lax.axis_index("line")
    lines, buses = ptdf.shape
    factors = chol.shape[0]
    half = nz // 2
    cut = buses // 2 // 128 * 128 + 128
    blocks = [(0, cut), (cut, buses - cut)]
    chip, core = me // 2, lax.rem(me, 2)
    row_of, col_of = chip // 4, lax.rem(chip, 4)
    z_order = [d for (d,) in far_first([(d,) for d in range(1, nz)], (nz,))]
    plane_order = far_first([(i, j) for i in range(4) for j in range(4) if i + j > 0], (4, 4))

    def chip_at(i, j):
        return lax.rem(row_of + i, 4) * 4 + lax.rem(col_of + j, 4)

    first = [(fob_h, fob), (gain_h, gain), (base_h, base)]
    later = [
        (rating_h, rating),
        (dirs_h, dirs),
        (shifts_h, shifts),
        (chol_h, chol),
        (mean_h, mean),
    ]
    pairs = list(first)
    for k, size in blocks:
        pairs.append((ptdf_h.at[:, pl.ds(k, size)], ptdf.at[:, pl.ds(k, size)]))
    pairs += later
    loads = [pltpu.make_async_copy(a, b, load_sem.at[i]) for i, (a, b) in enumerate(pairs)]
    for copy in loads:
        copy.start()

    barrier = pltpu.get_barrier_semaphore()

    reach = max(a - b for a, b in zip((half,) + LONG, LONG + (0,)))
    reach = max(reach, 3)
    for d in range(1, reach + 1):
        for peer in (lax.rem(z + d, nz), lax.rem(z + nz - d, nz)):
            pl.semaphore_signal(barrier, inc=1, device_id={"bus": peer}, device_id_type=MESH)
    for i, j in plane_order:
        pl.semaphore_signal(
            barrier,
            inc=1,
            device_id={"line": chip_at(i, j) * 2 + core},
            device_id_type=MESH,
        )
    pl.semaphore_signal(
        barrier, inc=1, device_id={"line": chip * 2 + 1 - core}, device_id_type=MESH
    )

    starts = [sum(WIDTHS[:p]) for p in range(PIECES)]

    def lanes(piece):
        return pl.ds(starts[piece], WIDTHS[piece])

    def columns(height):
        return lax.broadcasted_iota(jnp.int32, (height, 128), 0).astype(F32).astype(BF16)

    def spread(value, j, height):
        return jnp.broadcast_to(value[:, j : j + 128], (height, 128))

    def gather(piece):
        acc, wide = None, WIDTHS[piece]
        for i, (k, size) in enumerate(blocks):
            g_hi, g_lo = split(gain[pl.ds(k, size)].reshape(1, size))
            hi, lo = [], []
            for offset in range(0, wide, 256):
                height = min(256, wide - offset)
                nothing = jnp.zeros((height, 128), BF16)
                which = fob[pl.ds(k, size)].reshape(1, size) - (starts[piece] + offset)
                which = which.astype(F32).astype(BF16)
                hits = [columns(height) == spread(which, j, height) for j in range(0, size, 128)]
                for terms, value in ((hi, g_hi), (lo, g_lo)):
                    row = [
                        jnp.where(hits[j // 128], spread(value, j, height), nothing)
                        for j in range(0, size, 128)
                    ]
                    terms.append(jnp.concatenate(row, axis=1))
            stack = hi + lo
            if piece == 0:
                loads[len(first) + i].wait()
            if piece == 0:
                b_hi, b_lo = split(base[pl.ds(k, size)].reshape(1, size))
                stack.append(
                    jnp.concatenate(
                        [b_hi.astype(F32), b_lo.astype(F32), jnp.zeros((14, size), F32)], axis=0
                    ).astype(BF16)
                )
            part = dot(jnp.concatenate(stack, axis=0), ptdf[:, pl.ds(k, size)], NT)
            acc = part if acc is None else acc + part
        by_line = jnp.transpose(acc[0:wide] + acc[wide : 2 * wide])
        m_all[:, :, lanes(piece)] = by_line.reshape(nz, lines // nz, wide)
        if piece == 0:
            total_row = acc[2 * wide : 2 * wide + 1] + acc[2 * wide + 1 : 2 * wide + 2]
            base_row[0] = total_row[:, 0 : lines // 2]
            base_row[1] = total_row[:, lines // 2 :]

    def piece_of(piece, long_sign, start, land):
        sides = (
            (long_sign, LONG, half, 0 if long_sign > 0 else 1),
            (-long_sign, SHORT, half - 1, 0 if long_sign < 0 else 1),
        )
        return piece, sides, start, land

    pieces = [
        piece_of(
            p,
            1 if p == 0 else -1,
            lambda d, p=p: m_all.at[d, :, lanes(p)],
            lambda way, k, p=p: ring.at[way, k, :, lanes(p)],
        )
        for p in range(PIECES)
    ]
    pieces.append(
        piece_of(
            PIECES, -1, lambda d: base_row.at[d // (nz // 2)], lambda way, k: base_in.at[way, k]
        )
    )

    def toward(sign, k):
        return lax.rem(z + sign * k + nz, nz)

    def hop(piece, side, k, source):
        index, _, _, land = piece
        sign, stops, _, way = side
        return pltpu.make_async_remote_copy(
            src_ref=source,
            dst_ref=land(way, k),
            send_sem=ring_s.at[index, way, k],
            recv_sem=ring_r.at[index, way, k],
            device_id={"bus": toward(sign, k - next_stop(stops, k))},
            device_id_type=MESH,
        )

    def arrived(piece, side, k):
        hop(piece, side, k, piece[3](side[3], k)).wait_recv()

    sent = []

    def direct(piece, level):
        _, sides, start, _ = piece
        for k in range(half, 0, -1):
            for side in sides:
                sign, stops, far, _ = side
                if k <= far and k not in stops and next_stop(stops, k) == stops[level]:
                    copy = hop(piece, side, k, start(toward(sign, k)))
                    copy.start()
                    sent.append(copy)

    def merge(piece, level):
        _, sides, start, land = piece
        for side in sides:
            sign, stops, far, way = side
            c = stops[level]
            members = [k for k in range(far, 0, -1) if next_stop(stops, k) == c]
            block = start(toward(sign, c))[...]
            for k in members:
                arrived(piece, side, k)
                block = block + land(way, k)[...]
            land(way, members[0])[...] = block
            copy = hop(piece, side, c, land(way, members[0]))
            copy.start()
            sent.append(copy)

    def collect(piece):
        _, sides, start, land = piece
        block = start(z)[...]
        for side in sides:
            for k in range(side[2], 0, -1):
                if next_stop(side[1], k) == 0:
                    arrived(piece, side, k)
                    block = block + land(side[3], k)[...]
        return block

    def prepare():
        for copy in loads[len(first) + len(blocks) :]:
            copy.wait()
        point = lax.broadcasted_iota(jnp.int32, (POINTS, factors), 0)
        digits = jnp.zeros((POINTS, factors), jnp.int32)
        for bit in range(7):
            picked = lax.shift_right_logical(point, bit) & 1
            digits = digits ^ (picked * dirs[bit : bit + 1, :])
        table[...] = digits
        hi, lo = split(chol[...])
        c_hi[...] = hi
        c_lo[...] = lo

    def shadow(t):
        rows = pl.ds(t * POINTS, POINTS)
        normal = draw(table[...] ^ shifts[t : t + 1, :])
        hi, lo = split(normal)
        n_hi[rows, :] = hi
        n_lo[rows, :] = lo
        m_hi, m_lo = split(mean[...].reshape(1, factors))
        both = jnp.concatenate(
            [m_hi.astype(F32), m_lo.astype(F32), jnp.zeros((14, factors), F32)], axis=0
        ).astype(BF16)
        first = dot(both, hi, NT)
        second = dot(both, lo, NT)
        lik[t : t + 1, :] = jnp.exp(-(first[0:1, :] + (first[1:2, :] + second[0:1, :])))

    for copy in loads[: len(first)]:
        copy.wait()
    gather(0)
    pl.semaphore_wait(barrier, 2 * reach + nl // 2)
    direct(pieces[0], 0)
    direct(pieces[PIECES], 0)
    direct(pieces[0], 1)
    gather(1)
    direct(pieces[1], 0)
    direct(pieces[1], 1)
    direct(pieces[PIECES], 1)
    prepare()
    for level in range(len(LONG)):
        for t in GAPS[level]:
            shadow(t)
        if level < len(LONG) - 1:
            for piece in pieces:
                merge(piece, level)
        if level == 0:
            for piece in pieces:
                direct(piece, 2)

    own_lines = lines // nz
    base_line = collect(pieces[PIECES])
    base_line = jnp.concatenate([base_line, base_line], axis=1)
    mine = lax.broadcasted_iota(jnp.int32, (own_lines, lines), 1) == (
        lax.broadcasted_iota(jnp.int32, (own_lines, lines), 0) + z * own_lines
    )
    base_col = jnp.sum(jnp.where(mine, base_line, 0.0), axis=1, keepdims=True)
    rate_col = jnp.sum(jnp.where(mine, rating[...].reshape(1, lines).astype(F32) * 0.01, 0.0), axis=1, keepdims=True)
    steep = SHARP / rate_col

    total_m = jnp.concatenate([collect(pieces[p]) for p in range(PIECES)], axis=1)

    h, l = split(total_m)
    g = dot(h, c_hi[...], NN) + (dot(l, c_hi[...], NN) + dot(h, c_lo[...], NN))
    const = jnp.sum(g * mean[...].reshape(1, factors), axis=1, keepdims=True) + base_col
    gh, gl = split(g)
    both = jnp.concatenate([gh.astype(F32), gl.astype(F32)], axis=0).astype(BF16)
    low_lane = lax.broadcasted_iota(jnp.int32, (8, POINTS), 1) < POINTS // 2
    for k in range(8):
        rows = pl.ds(k * POINTS, POINTS)
        first = dot(both, n_hi[rows, :], NT)
        second = dot(gh, n_lo[rows, :], NT)
        x = first[0:own_lines, :] + (first[own_lines:, :] + second) + const
        v = jnp.abs(x) * steep - SHARP
        soft = jnp.maximum(v, 0.0) + jnp.log1p(jnp.exp(-jnp.abs(v)))
        share[k : k + 1, :] = jnp.sum(soft, axis=0, keepdims=True) * (1.0 / (SHARP * lines * nl))
        top, low = x[0:8, :], x[8:16, :]
        send[2 * k] = jnp.where(low_lane, top, pltpu.roll(low, POINTS // 2, 1))
        send[2 * k + 1] = jnp.where(low_lane, pltpu.roll(top, POINTS // 2, 1), low)

    def send_to(source, slots, slot, send_sem, recv_sem, axis, peer):
        return pltpu.make_async_remote_copy(
            src_ref=source,
            dst_ref=slots.at[slot],
            send_sem=send_sem,
            recv_sem=recv_sem,
            device_id={axis: peer},
            device_id_type=MESH,
        )

    partner = pltpu.make_async_remote_copy(
        src_ref=share,
        dst_ref=pair_in,
        send_sem=cs,
        recv_sem=cr,
        device_id={"line": chip * 2 + 1 - core},
        device_id_type=MESH,
    )
    partner.start()
    recv[z] = send[z]
    partner.wait_recv()
    chip_sum[...] = share[...] + pair_in[...]

    def plane_copy(n, slot):
        peer = chip_at(*plane_order[n])
        slot = chip if slot is None else peer
        return send_to(chip_sum, plane_in, slot, ls.at[n], lr.at[slot], "line", peer * 2 + core)

    def flow_copy(d, slot):
        peer = lax.rem(z + d, nz)
        slot = z if slot is None else peer
        return send_to(send.at[peer], recv, slot, fs.at[d], fr.at[slot], "bus", peer)

    def deep_copy(d, slot):
        peer = lax.rem(z + d, nz)
        slot = z if slot is None else peer
        return send_to(plane_sum, deep_in, slot, ds.at[d], dr.at[slot], "bus", peer)

    for n in range(len(plane_order)):
        copy = plane_copy(n, None)
        copy.start()
        sent.append(copy)
    for d in z_order:
        copy = flow_copy(d, None)
        copy.start()
        sent.append(copy)
    plane_in[chip] = chip_sum[...]
    for n in range(len(plane_order)):
        plane_copy(n, n).wait_recv()
    partial = plane_in[0]
    for j in range(1, nl // 2):
        partial = partial + plane_in[j]
    plane_sum[...] = partial
    for d in z_order:
        copy = deep_copy(d, None)
        copy.start()
        sent.append(copy)
    deep_in[z] = partial

    for d in z_order:
        flow_copy(d, d).wait_recv()
    tiles = []
    for j in range(nz):
        tile = recv[j]
        tiles.append(tile)
        tiles.append(pltpu.roll(tile, POINTS // 2, 1))
    by_line = jnp.concatenate(tiles, axis=0)
    flows_o[...] = jnp.transpose(by_line)[0 : POINTS // 2, :]

    for d in z_order:
        deep_copy(d, d).wait_recv()
    total_over = deep_in[0]
    for j in range(1, nz):
        total_over = total_over + deep_in[j]
    over[...] = total_over
    emphasis = lik[...] * total_over
    total = jnp.sum(jnp.sum(emphasis, axis=1, keepdims=True), axis=0, keepdims=True)
    inverse = 1.0 / total
    flat = jnp.concatenate([emphasis[k : k + 1, :] for k in range(8)], axis=1)
    e_hi, e_lo = split(flat)
    both = jnp.concatenate(
        [e_hi.astype(F32), e_lo.astype(F32), jnp.zeros((14, flat.shape[1]), F32)], axis=0
    ).astype(BF16)
    first = dot(both, n_hi[...], NN)
    second = dot(both, n_lo[...], NN)
    moved = first[0:1, :] + (first[1:2, :] + second[0:1, :])
    newmean_o[...] = mean[...].reshape(1, factors) + moved * inverse
    row = over[pl.ds(z // 2, 1), :]
    like_row = lik[pl.ds(z // 2, 1), :]
    odd = lax.rem(z, 2) == 1
    row = jnp.where(odd, row[:, POINTS // 2 :], row[:, 0 : POINTS // 2])
    like_row = jnp.where(odd, like_row[:, POINTS // 2 :], like_row[:, 0 : POINTS // 2])
    overload_o[...] = row
    weight_o[...] = (float(8 * POINTS) * like_row) * row * inverse

    partner.wait_send()
    for copy in sent:
        copy.wait_send()


def deliver(*refs):
    sources, targets, sem = refs[0:4], refs[4:8], refs[8]
    copies = []
    for i, (source, target) in enumerate(zip(sources, targets)):
        if len(target.shape) == 1:
            source = source.at[0]
        copies.append(pltpu.make_async_copy(source, target, sem.at[i]))
    for copy in copies:
        copy.start()
    for copy in copies:
        copy.wait()


def per_device(nz, nl, ptdf, base, gain, fob, rating, dirs, shifts, chol, mean):
    lines, buses = ptdf.shape
    factors = chol.shape[0]
    half = nz // 2
    own = lines // nz
    scen = shifts.shape[0] * POINTS
    vm, dma = pltpu.VMEM, pltpu.SemaphoreType.DMA
    anywhere = pl.BlockSpec(memory_space=pl.ANY)
    inside = pl.BlockSpec(memory_space=pltpu.VMEM)
    n_loads = 10
    flows, overload, weight, new_mean = pl.pallas_call(
        functools.partial(kernel, nz, nl),
        out_shape=(
            jax.ShapeDtypeStruct((scen // nz, lines), F32),
            jax.ShapeDtypeStruct((1, scen // nz), F32),
            jax.ShapeDtypeStruct((1, scen // nz), F32),
            jax.ShapeDtypeStruct((1, factors), F32),
        ),
        in_specs=[anywhere] * 9,
        out_specs=(inside,) * 4,
        scratch_shapes=[
            vm((lines, buses), BF16),
            vm((buses,), F32),
            vm((buses,), F32),
            vm((buses,), jnp.int32),
            vm((lines,), jnp.int32),
            vm(dirs.shape, jnp.int32),
            vm(shifts.shape, jnp.int32),
            vm(chol.shape, F32),
            vm((factors,), F32),
            vm((nz, own, factors), F32),
            vm((2, half + 1, own, factors), F32),
            vm((POINTS, factors), jnp.int32),
            vm((scen, factors), BF16),
            vm((scen, factors), BF16),
            vm(chol.shape, BF16),
            vm(chol.shape, BF16),
            vm((8, POINTS), F32),
            vm((2, 1, POINTS), F32),
            vm((2, half + 1, 1, POINTS), F32),
            vm((nz, 8, POINTS), F32),
            vm((nz, 8, POINTS), F32),
            vm((8, POINTS), F32),
            vm((8, POINTS), F32),
            vm((8, POINTS), F32),
            vm((nl // 2, 8, POINTS), F32),
            vm((8, POINTS), F32),
            vm((nz, 8, POINTS), F32),
            vm((8, POINTS), F32),
            dma((n_loads,)),
            dma((PIECES + 1, 2, half + 1)),
            dma((PIECES + 1, 2, half + 1)),
            dma((nz,)),
            dma((nz,)),
            dma(()),
            dma(()),
            dma((nl // 2,)),
            dma((nl // 2,)),
            dma((nz,)),
            dma((nz,)),
        ],
        compiler_params=pltpu.CompilerParams(
            collective_id=0, has_side_effects=True, vmem_limit_bytes=40 * 1024 * 1024
        ),
    )(
        *[
            pltpu.with_memory_space_constraint(a, pltpu.HBM)
            for a in (ptdf, base, gain, fob, rating, dirs, shifts, chol, mean)
        ]
    )
    results = (flows, overload, weight, new_mean)
    return pl.pallas_call(
        deliver,
        out_shape=tuple(jax.ShapeDtypeStruct(a.shape if a.shape[0] > 1 else a.shape[1:], F32) for a in results),
        in_specs=[pl.BlockSpec(memory_space=pltpu.VMEM)] * 4,
        out_specs=(anywhere,) * 4,
        scratch_shapes=[dma((4,))],
        compiler_params=pltpu.CompilerParams(vmem_limit_bytes=1024 * 1024),
    )(*results)


def solution(mesh):
    nz, nl = mesh.shape["bus"], mesh.shape["line"]
    return jax.shard_map(
        functools.partial(per_device, nz, nl),
        mesh=mesh,
        in_specs=(P("line", "bus"), P("bus"), P("bus"), P("bus"), P("line"), P(), P(), P(), P()),
        out_specs=(P("bus", "line"), P("bus"), P("bus"), P()),
        check_vma=False,
    )
```

```python
import functools
import math

import jax
import jax.numpy as jnp
from jax import lax
from jax.experimental import pallas as pl
from jax.experimental.pallas import tpu as pltpu
from jax.sharding import PartitionSpec as P

MESH = pl.DeviceIdType.MESH
POINTS = 128
SHARP = 8.0
F32 = jnp.float32
BF16 = jnp.bfloat16
NT = (((1,), (1,)), ((), ()))
NN = (((1,), (0,)), ((), ()))
WIDTHS = (256, 256)
PIECES = len(WIDTHS)
BLOCK = 3072
LONG = (6, 3, 0)
SHORT = (5, 2, 0)
GAPS = ((0, 2), (2, 5), (5, 8))

CENTRAL = (
    2.81022636e-08,
    3.43273939e-07,
    -3.5233877e-06,
    -4.39150654e-06,
    0.00021858087,
    -0.00125372503,
    -0.00417768164,
    0.246640727,
    1.50140941,
)
TAIL = (
    -0.000200214257,
    0.000100950558,
    0.00134934322,
    -0.00367342844,
    0.00573950773,
    -0.0076224613,
    0.00943887047,
    1.00167406,
    2.83297682,
)


def dot(a, b, dims):
    return lax.dot_general(a, b, dims, preferred_element_type=F32)


def split(x):
    hi = x.astype(BF16)
    return hi, (x - hi.astype(F32)).astype(BF16)


def draw(digits):
    x = (2 * lax.shift_right_arithmetic(digits, 7) + 1).astype(F32) * (1.0 / 8388608.0) - 1.0
    w = -jnp.log((1.0 - x) * (1.0 + x))
    near = w < 5.0
    t = jnp.where(near, w - 2.5, jnp.sqrt(w) - 3.0)
    p = jnp.where(near, CENTRAL[0], TAIL[0])
    for a, b in zip(CENTRAL[1:], TAIL[1:]):
        p = jnp.where(near, a, b) + p * t
    return math.sqrt(2.0) * x * p


def next_stop(stops, k):
    return max(c for c in stops if c < k)


def far_first(offsets, sizes):
    reach = [sum(min(o, n - o) for o, n in zip(off, sizes)) for off in offsets]
    return [offsets[i] for i in sorted(range(len(offsets)), key=lambda i: -reach[i])]


def kernel(
    nz,
    nl,
    ptdf_h,
    base_h,
    gain_h,
    fob_h,
    rating_h,
    dirs_h,
    shifts_h,
    chol_h,
    mean_h,
    flows_o,
    overload_o,
    weight_o,
    newmean_o,
    ptdf,
    base,
    gain,
    fob,
    rating,
    dirs,
    shifts,
    chol,
    mean,
    m_all,
    totals,
    ring,
    table,
    n_hi,
    n_lo,
    c_hi,
    c_lo,
    lik,
    base_row,
    base_in,
    send,
    recv,
    share,
    pair_in,
    chip_sum,
    plane_in,
    plane_sum,
    deep_in,
    over,
    load_sem,
    ring_s,
    ring_r,
    fs,
    fr,
    cs,
    cr,
    ls,
    lr,
    ds,
    dr,
):
    z = lax.axis_index("bus")
    me = lax.axis_index("line")
    lines, buses = ptdf.shape
    factors = chol.shape[0]
    half = nz // 2
    full = buses // BLOCK
    rest = buses - full * BLOCK
    blocks = [(k, min(BLOCK, buses - k)) for k in range(0, buses, BLOCK)]
    chip, core = me // 2, lax.rem(me, 2)
    row_of, col_of = chip // 4, lax.rem(chip, 4)
    z_order = [d for (d,) in far_first([(d,) for d in range(1, nz)], (nz,))]
    plane_order = far_first([(i, j) for i in range(4) for j in range(4) if i + j > 0], (4, 4))

    def chip_at(i, j):
        return lax.rem(row_of + i, 4) * 4 + lax.rem(col_of + j, 4)

    first = [(fob_h, fob), (gain_h, gain), (base_h, base)]
    later = [
        (rating_h, rating),
        (dirs_h, dirs),
        (shifts_h, shifts),
        (chol_h, chol),
        (mean_h, mean),
    ]
    pairs = list(first)
    for k, size in blocks:
        pairs.append((ptdf_h.at[:, pl.ds(k, size)], ptdf.at[:, pl.ds(k, size)]))
    pairs += later
    loads = [pltpu.make_async_copy(a, b, load_sem.at[i]) for i, (a, b) in enumerate(pairs)]
    for copy in loads:
        copy.start()

    barrier = pltpu.get_barrier_semaphore()

    reach = max(a - b for a, b in zip((half,) + LONG, LONG + (0,)))
    reach = max(reach, 3)
    for d in range(1, reach + 1):
        for peer in (lax.rem(z + d, nz), lax.rem(z + nz - d, nz)):
            pl.semaphore_signal(barrier, inc=1, device_id={"bus": peer}, device_id_type=MESH)
    for i, j in plane_order:
        pl.semaphore_signal(
            barrier,
            inc=1,
            device_id={"line": chip_at(i, j) * 2 + core},
            device_id_type=MESH,
        )
    pl.semaphore_signal(
        barrier, inc=1, device_id={"line": chip * 2 + 1 - core}, device_id_type=MESH
    )

    starts = [sum(WIDTHS[:p]) for p in range(PIECES)]

    def lanes(piece):
        return pl.ds(starts[piece], WIDTHS[piece])

    def columns(height):
        return lax.broadcasted_iota(jnp.int32, (height, 128), 0).astype(F32).astype(BF16)

    def spread(value, j, height):
        return jnp.broadcast_to(value[:, j : j + 128], (height, 128))

    def gather(piece):
        wide = WIDTHS[piece]
        height = 2 * wide + (16 if piece == 0 else 0)
        nothing = jnp.zeros((wide, 128), BF16)

        def product(k, size, index):
            g_hi, g_lo = split(gain[pl.ds(k, size)].reshape(1, size))
            which = (fob[pl.ds(k, size)].reshape(1, size) - starts[piece]).astype(F32).astype(BF16)
            hits = [columns(wide) == spread(which, j, wide) for j in range(0, size, 128)]
            stack = []
            for value in (g_hi, g_lo):
                row = [
                    jnp.where(hits[j // 128], spread(value, j, wide), nothing)
                    for j in range(0, size, 128)
                ]
                stack.append(jnp.concatenate(row, axis=1))
            if piece == 0:
                b_hi, b_lo = split(base[pl.ds(k, size)].reshape(1, size))
                stack.append(
                    jnp.concatenate(
                        [b_hi.astype(F32), b_lo.astype(F32), jnp.zeros((14, size), F32)], axis=0
                    ).astype(BF16)
                )
                pltpu.make_async_copy(
                    ptdf_h.at[:, pl.ds(k, size)],
                    ptdf.at[:, pl.ds(k, size)],
                    load_sem.at[len(first) + index],
                ).wait()
            return dot(jnp.concatenate(stack, axis=0), ptdf[:, pl.ds(k, size)], NT)

        def step(i, carry):
            totals[0:height] += product(pl.multiple_of(i * BLOCK, BLOCK), BLOCK, i)
            return carry

        totals[0:height] = jnp.zeros((height, lines), F32)
        lax.fori_loop(0, full, step, 0)
        acc = totals[0:height]
        if rest:
            acc = acc + product(full * BLOCK, rest, full)
        by_line = jnp.transpose(acc[0:wide] + acc[wide : 2 * wide])
        m_all[:, :, lanes(piece)] = by_line.reshape(nz, lines // nz, wide)
        if piece == 0:
            total_row = acc[2 * wide : 2 * wide + 1] + acc[2 * wide + 1 : 2 * wide + 2]
            base_row[0] = total_row[:, 0 : lines // 2]
            base_row[1] = total_row[:, lines // 2 :]

    def piece_of(piece, long_sign, start, land):
        sides = (
            (long_sign, LONG, half, 0 if long_sign > 0 else 1),
            (-long_sign, SHORT, half - 1, 0 if long_sign < 0 else 1),
        )
        return piece, sides, start, land

    pieces = [
        piece_of(
            p,
            1 if p == 0 else -1,
            lambda d, p=p: m_all.at[d, :, lanes(p)],
            lambda way, k, p=p: ring.at[way, k, :, lanes(p)],
        )
        for p in range(PIECES)
    ]
    pieces.append(
        piece_of(
            PIECES, -1, lambda d: base_row.at[d // (nz // 2)], lambda way, k: base_in.at[way, k]
        )
    )

    def toward(sign, k):
        return lax.rem(z + sign * k + nz, nz)

    def hop(piece, side, k, source):
        index, _, _, land = piece
        sign, stops, _, way = side
        return pltpu.make_async_remote_copy(
            src_ref=source,
            dst_ref=land(way, k),
            send_sem=ring_s.at[index, way, k],
            recv_sem=ring_r.at[index, way, k],
            device_id={"bus": toward(sign, k - next_stop(stops, k))},
            device_id_type=MESH,
        )

    def arrived(piece, side, k):
        hop(piece, side, k, piece[3](side[3], k)).wait_recv()

    sent = []

    def direct(piece, level):
        _, sides, start, _ = piece
        for k in range(half, 0, -1):
            for side in sides:
                sign, stops, far, _ = side
                if k <= far and k not in stops and next_stop(stops, k) == stops[level]:
                    copy = hop(piece, side, k, start(toward(sign, k)))
                    copy.start()
                    sent.append(copy)

    def merge(piece, level):
        _, sides, start, land = piece
        for side in sides:
            sign, stops, far, way = side
            c = stops[level]
            members = [k for k in range(far, 0, -1) if next_stop(stops, k) == c]
            block = start(toward(sign, c))[...]
            for k in members:
                arrived(piece, side, k)
                block = block + land(way, k)[...]
            land(way, members[0])[...] = block
            copy = hop(piece, side, c, land(way, members[0]))
            copy.start()
            sent.append(copy)

    def collect(piece):
        _, sides, start, land = piece
        block = start(z)[...]
        for side in sides:
            for k in range(side[2], 0, -1):
                if next_stop(side[1], k) == 0:
                    arrived(piece, side, k)
                    block = block + land(side[3], k)[...]
        return block

    def prepare():
        for copy in loads[len(first) + len(blocks) :]:
            copy.wait()
        point = lax.broadcasted_iota(jnp.int32, (POINTS, factors), 0)
        digits = jnp.zeros((POINTS, factors), jnp.int32)
        for bit in range(7):
            picked = lax.shift_right_logical(point, bit) & 1
            digits = digits ^ (picked * dirs[bit : bit + 1, :])
        table[...] = digits
        hi, lo = split(chol[...])
        c_hi[...] = hi
        c_lo[...] = lo

    def shadow(t, carry):
        rows = pl.ds(pl.multiple_of(t * POINTS, POINTS), POINTS)
        normal = draw(table[...] ^ shifts[pl.ds(t, 1), :])
        hi, lo = split(normal)
        n_hi[rows, :] = hi
        n_lo[rows, :] = lo
        m_hi, m_lo = split(mean[...].reshape(1, factors))
        both = jnp.concatenate(
            [m_hi.astype(F32), m_lo.astype(F32), jnp.zeros((14, factors), F32)], axis=0
        ).astype(BF16)
        first = dot(both, hi, NT)
        second = dot(both, lo, NT)
        lik[pl.ds(t, 1), :] = jnp.exp(-(first[0:1, :] + (first[1:2, :] + second[0:1, :])))
        return carry

    for copy in loads[: len(first)]:
        copy.wait()
    gather(0)
    pl.semaphore_wait(barrier, 2 * reach + nl // 2)
    direct(pieces[0], 0)
    direct(pieces[PIECES], 0)
    direct(pieces[0], 1)
    gather(1)
    direct(pieces[1], 0)
    direct(pieces[1], 1)
    direct(pieces[PIECES], 1)
    prepare()
    for level in range(len(LONG)):
        lax.fori_loop(GAPS[level][0], GAPS[level][1], shadow, 0)
        if level < len(LONG) - 1:
            for piece in pieces:
                merge(piece, level)
        if level == 0:
            for piece in pieces:
                direct(piece, 2)

    own_lines = lines // nz
    base_line = collect(pieces[PIECES])
    base_line = jnp.concatenate([base_line, base_line], axis=1)
    mine = lax.broadcasted_iota(jnp.int32, (own_lines, lines), 1) == (
        lax.broadcasted_iota(jnp.int32, (own_lines, lines), 0) + z * own_lines
    )
    base_col = jnp.sum(jnp.where(mine, base_line, 0.0), axis=1, keepdims=True)
    rate_col = jnp.sum(jnp.where(mine, rating[...].reshape(1, lines).astype(F32) * 0.01, 0.0), axis=1, keepdims=True)
    steep = SHARP / rate_col

    total_m = jnp.concatenate([collect(pieces[p]) for p in range(PIECES)], axis=1)

    h, l = split(total_m)
    g = dot(h, c_hi[...], NN) + (dot(l, c_hi[...], NN) + dot(h, c_lo[...], NN))
    const = jnp.sum(g * mean[...].reshape(1, factors), axis=1, keepdims=True) + base_col
    gh, gl = split(g)
    both = jnp.concatenate([gh.astype(F32), gl.astype(F32)], axis=0).astype(BF16)
    low_lane = lax.broadcasted_iota(jnp.int32, (8, POINTS), 1) < POINTS // 2
    for k in range(8):
        rows = pl.ds(k * POINTS, POINTS)
        first = dot(both, n_hi[rows, :], NT)
        second = dot(gh, n_lo[rows, :], NT)
        x = first[0:own_lines, :] + (first[own_lines:, :] + second) + const
        v = jnp.abs(x) * steep - SHARP
        soft = jnp.maximum(v, 0.0) + jnp.log1p(jnp.exp(-jnp.abs(v)))
        share[k : k + 1, :] = jnp.sum(soft, axis=0, keepdims=True) * (1.0 / (SHARP * lines * nl))
        top, low = x[0:8, :], x[8:16, :]
        send[2 * k] = jnp.where(low_lane, top, pltpu.roll(low, POINTS // 2, 1))
        send[2 * k + 1] = jnp.where(low_lane, pltpu.roll(top, POINTS // 2, 1), low)

    def send_to(source, slots, slot, send_sem, recv_sem, axis, peer):
        return pltpu.make_async_remote_copy(
            src_ref=source,
            dst_ref=slots.at[slot],
            send_sem=send_sem,
            recv_sem=recv_sem,
            device_id={axis: peer},
            device_id_type=MESH,
        )

    partner = pltpu.make_async_remote_copy(
        src_ref=share,
        dst_ref=pair_in,
        send_sem=cs,
        recv_sem=cr,
        device_id={"line": chip * 2 + 1 - core},
        device_id_type=MESH,
    )
    partner.start()
    recv[z] = send[z]
    partner.wait_recv()
    chip_sum[...] = share[...] + pair_in[...]

    def plane_copy(n, slot):
        peer = chip_at(*plane_order[n])
        slot = chip if slot is None else peer
        return send_to(chip_sum, plane_in, slot, ls.at[n], lr.at[slot], "line", peer * 2 + core)

    def flow_copy(d, slot):
        peer = lax.rem(z + d, nz)
        slot = z if slot is None else peer
        return send_to(send.at[peer], recv, slot, fs.at[d], fr.at[slot], "bus", peer)

    def deep_copy(d, slot):
        peer = lax.rem(z + d, nz)
        slot = z if slot is None else peer
        return send_to(plane_sum, deep_in, slot, ds.at[d], dr.at[slot], "bus", peer)

    for n in range(len(plane_order)):
        copy = plane_copy(n, None)
        copy.start()
        sent.append(copy)
    for d in z_order:
        copy = flow_copy(d, None)
        copy.start()
        sent.append(copy)
    plane_in[chip] = chip_sum[...]
    for n in range(len(plane_order)):
        plane_copy(n, n).wait_recv()
    partial = plane_in[0]
    for j in range(1, nl // 2):
        partial = partial + plane_in[j]
    plane_sum[...] = partial
    for d in z_order:
        copy = deep_copy(d, None)
        copy.start()
        sent.append(copy)
    deep_in[z] = partial

    for d in z_order:
        flow_copy(d, d).wait_recv()
    tiles = []
    for j in range(nz):
        tile = recv[j]
        tiles.append(tile)
        tiles.append(pltpu.roll(tile, POINTS // 2, 1))
    by_line = jnp.concatenate(tiles, axis=0)
    flows_o[...] = jnp.transpose(by_line)[0 : POINTS // 2, :]

    for d in z_order:
        deep_copy(d, d).wait_recv()
    total_over = deep_in[0]
    for j in range(1, nz):
        total_over = total_over + deep_in[j]
    over[...] = total_over
    emphasis = lik[...] * total_over
    total = jnp.sum(jnp.sum(emphasis, axis=1, keepdims=True), axis=0, keepdims=True)
    inverse = 1.0 / total
    flat = jnp.concatenate([emphasis[k : k + 1, :] for k in range(8)], axis=1)
    e_hi, e_lo = split(flat)
    both = jnp.concatenate(
        [e_hi.astype(F32), e_lo.astype(F32), jnp.zeros((14, flat.shape[1]), F32)], axis=0
    ).astype(BF16)
    first = dot(both, n_hi[...], NN)
    second = dot(both, n_lo[...], NN)
    moved = first[0:1, :] + (first[1:2, :] + second[0:1, :])
    newmean_o[...] = mean[...].reshape(1, factors) + moved * inverse
    row = over[pl.ds(z // 2, 1), :]
    like_row = lik[pl.ds(z // 2, 1), :]
    odd = lax.rem(z, 2) == 1
    row = jnp.where(odd, row[:, POINTS // 2 :], row[:, 0 : POINTS // 2])
    like_row = jnp.where(odd, like_row[:, POINTS // 2 :], like_row[:, 0 : POINTS // 2])
    overload_o[...] = row
    weight_o[...] = (float(8 * POINTS) * like_row) * row * inverse

    partner.wait_send()
    for copy in sent:
        copy.wait_send()


def deliver(*refs):
    sources, targets, sem = refs[0:4], refs[4:8], refs[8]
    copies = []
    for i, (source, target) in enumerate(zip(sources, targets)):
        if len(target.shape) == 1:
            source = source.at[0]
        copies.append(pltpu.make_async_copy(source, target, sem.at[i]))
    for copy in copies:
        copy.start()
    for copy in copies:
        copy.wait()


def per_device(nz, nl, ptdf, base, gain, fob, rating, dirs, shifts, chol, mean):
    lines, buses = ptdf.shape
    factors = chol.shape[0]
    half = nz // 2
    own = lines // nz
    scen = shifts.shape[0] * POINTS
    vm, dma = pltpu.VMEM, pltpu.SemaphoreType.DMA
    anywhere = pl.BlockSpec(memory_space=pl.ANY)
    inside = pl.BlockSpec(memory_space=pltpu.VMEM)
    n_loads = 8 + -(-buses // BLOCK)
    flows, overload, weight, new_mean = pl.pallas_call(
        functools.partial(kernel, nz, nl),
        out_shape=(
            jax.ShapeDtypeStruct((scen // nz, lines), F32),
            jax.ShapeDtypeStruct((1, scen // nz), F32),
            jax.ShapeDtypeStruct((1, scen // nz), F32),
            jax.ShapeDtypeStruct((1, factors), F32),
        ),
        in_specs=[anywhere] * 9,
        out_specs=(inside,) * 4,
        scratch_shapes=[
            vm((lines, buses), BF16),
            vm((buses,), F32),
            vm((buses,), F32),
            vm((buses,), jnp.int32),
            vm((lines,), jnp.int32),
            vm(dirs.shape, jnp.int32),
            vm(shifts.shape, jnp.int32),
            vm(chol.shape, F32),
            vm((factors,), F32),
            vm((nz, own, factors), F32),
            vm((2 * max(WIDTHS) + 16, lines), F32),
            vm((2, half + 1, own, factors), F32),
            vm((POINTS, factors), jnp.int32),
            vm((scen, factors), BF16),
            vm((scen, factors), BF16),
            vm(chol.shape, BF16),
            vm(chol.shape, BF16),
            vm((8, POINTS), F32),
            vm((2, 1, POINTS), F32),
            vm((2, half + 1, 1, POINTS), F32),
            vm((nz, 8, POINTS), F32),
            vm((nz, 8, POINTS), F32),
            vm((8, POINTS), F32),
            vm((8, POINTS), F32),
            vm((8, POINTS), F32),
            vm((nl // 2, 8, POINTS), F32),
            vm((8, POINTS), F32),
            vm((nz, 8, POINTS), F32),
            vm((8, POINTS), F32),
            dma((n_loads,)),
            dma((PIECES + 1, 2, half + 1)),
            dma((PIECES + 1, 2, half + 1)),
            dma((nz,)),
            dma((nz,)),
            dma(()),
            dma(()),
            dma((nl // 2,)),
            dma((nl // 2,)),
            dma((nz,)),
            dma((nz,)),
        ],
        compiler_params=pltpu.CompilerParams(
            collective_id=0, has_side_effects=True, vmem_limit_bytes=40 * 1024 * 1024
        ),
    )(
        *[
            pltpu.with_memory_space_constraint(a, pltpu.HBM)
            for a in (ptdf, base, gain, fob, rating, dirs, shifts, chol, mean)
        ]
    )
    results = (flows, overload, weight, new_mean)
    return pl.pallas_call(
        deliver,
        out_shape=tuple(jax.ShapeDtypeStruct(a.shape if a.shape[0] > 1 else a.shape[1:], F32) for a in results),
        in_specs=[pl.BlockSpec(memory_space=pltpu.VMEM)] * 4,
        out_specs=(anywhere,) * 4,
        scratch_shapes=[dma((4,))],
        compiler_params=pltpu.CompilerParams(vmem_limit_bytes=1024 * 1024),
    )(*results)


def solution(mesh):
    nz, nl = mesh.shape["bus"], mesh.shape["line"]
    return jax.shard_map(
        functools.partial(per_device, nz, nl),
        mesh=mesh,
        in_specs=(P("line", "bus"), P("bus"), P("bus"), P("bus"), P("line"), P(), P(), P(), P()),
        out_specs=(P("bus", "line"), P("bus"), P("bus"), P()),
        check_vma=False,
    )
```

```python
import functools
import math

import jax
import jax.numpy as jnp
from jax import lax
from jax.experimental import pallas as pl
from jax.experimental.pallas import tpu as pltpu
from jax.sharding import PartitionSpec as P

MESH = pl.DeviceIdType.MESH
POINTS = 128
SHARP = 8.0
F32 = jnp.float32
BF16 = jnp.bfloat16
NT = (((1,), (1,)), ((), ()))
NN = (((1,), (0,)), ((), ()))
WIDTHS = (256, 256)
PIECES = len(WIDTHS)
BLOCK = 3200
LONG = (6, 3, 0)
SHORT = (5, 2, 0)
GAPS = ((0, 2), (2, 5), (5, 8))

CENTRAL = (
    2.81022636e-08,
    3.43273939e-07,
    -3.5233877e-06,
    -4.39150654e-06,
    0.00021858087,
    -0.00125372503,
    -0.00417768164,
    0.246640727,
    1.50140941,
)
TAIL = (
    -0.000200214257,
    0.000100950558,
    0.00134934322,
    -0.00367342844,
    0.00573950773,
    -0.0076224613,
    0.00943887047,
    1.00167406,
    2.83297682,
)


def dot(a, b, dims):
    return lax.dot_general(a, b, dims, preferred_element_type=F32)


def split(x):
    hi = x.astype(BF16)
    return hi, (x - hi.astype(F32)).astype(BF16)


def draw(digits):
    x = (2 * lax.shift_right_arithmetic(digits, 7) + 1).astype(F32) * (1.0 / 8388608.0) - 1.0
    w = -jnp.log((1.0 - x) * (1.0 + x))
    near = w < 5.0
    t = jnp.where(near, w - 2.5, jnp.sqrt(w) - 3.0)
    p = jnp.where(near, CENTRAL[0], TAIL[0])
    for a, b in zip(CENTRAL[1:], TAIL[1:]):
        p = jnp.where(near, a, b) + p * t
    return math.sqrt(2.0) * x * p


def next_stop(stops, k):
    return max(c for c in stops if c < k)


def far_first(offsets, sizes):
    reach = [sum(min(o, n - o) for o, n in zip(off, sizes)) for off in offsets]
    return [offsets[i] for i in sorted(range(len(offsets)), key=lambda i: -reach[i])]


def kernel(
    nz,
    nl,
    ptdf_h,
    base_h,
    gain_h,
    fob_h,
    rating_h,
    dirs_h,
    shifts_h,
    chol_h,
    mean_h,
    flows_o,
    overload_o,
    weight_o,
    newmean_o,
    ptdf,
    base,
    gain,
    fob,
    rating,
    dirs,
    shifts,
    chol,
    mean,
    m_all,
    totals,
    ring,
    table,
    n_hi,
    n_lo,
    c_hi,
    c_lo,
    lik,
    base_row,
    base_in,
    send,
    recv,
    share,
    pair_in,
    chip_sum,
    plane_in,
    plane_sum,
    deep_in,
    over,
    load_sem,
    ring_s,
    ring_r,
    fs,
    fr,
    cs,
    cr,
    ls,
    lr,
    ds,
    dr,
):
    z = lax.axis_index("bus")
    me = lax.axis_index("line")
    lines, buses = ptdf.shape
    factors = chol.shape[0]
    half = nz // 2
    full = -(-buses // BLOCK)
    overlap = full * BLOCK - buses
    stride = BLOCK - overlap
    blocks = [(0, BLOCK), (BLOCK, buses - BLOCK)]
    chip, core = me // 2, lax.rem(me, 2)
    row_of, col_of = chip // 4, lax.rem(chip, 4)
    z_order = [d for (d,) in far_first([(d,) for d in range(1, nz)], (nz,))]
    plane_order = far_first([(i, j) for i in range(4) for j in range(4) if i + j > 0], (4, 4))

    def chip_at(i, j):
        return lax.rem(row_of + i, 4) * 4 + lax.rem(col_of + j, 4)

    first = [(fob_h, fob), (gain_h, gain), (base_h, base)]
    later = [
        (rating_h, rating),
        (dirs_h, dirs),
        (shifts_h, shifts),
        (chol_h, chol),
        (mean_h, mean),
    ]
    pairs = list(first)
    for k, size in blocks:
        pairs.append((ptdf_h.at[:, pl.ds(k, size)], ptdf.at[:, pl.ds(k, size)]))
    pairs += later
    loads = [pltpu.make_async_copy(a, b, load_sem.at[i]) for i, (a, b) in enumerate(pairs)]
    for copy in loads:
        copy.start()

    barrier = pltpu.get_barrier_semaphore()

    reach = max(a - b for a, b in zip((half,) + LONG, LONG + (0,)))
    reach = max(reach, 3)
    for d in range(1, reach + 1):
        for peer in (lax.rem(z + d, nz), lax.rem(z + nz - d, nz)):
            pl.semaphore_signal(barrier, inc=1, device_id={"bus": peer}, device_id_type=MESH)
    for i, j in plane_order:
        pl.semaphore_signal(
            barrier,
            inc=1,
            device_id={"line": chip_at(i, j) * 2 + core},
            device_id_type=MESH,
        )
    pl.semaphore_signal(
        barrier, inc=1, device_id={"line": chip * 2 + 1 - core}, device_id_type=MESH
    )

    starts = [sum(WIDTHS[:p]) for p in range(PIECES)]

    def lanes(piece):
        return pl.ds(starts[piece], WIDTHS[piece])

    def columns(height):
        return lax.broadcasted_iota(jnp.int32, (height, 128), 0).astype(F32).astype(BF16)

    def spread(value, j, height):
        return jnp.broadcast_to(value[:, j : j + 128], (height, 128))

    def gather(piece):
        wide = WIDTHS[piece]
        height = 2 * wide + (16 if piece == 0 else 0)
        nothing = jnp.zeros((wide, 128), BF16)

        def product(k, size, index):
            fresh = (lax.broadcasted_iota(jnp.int32, (1, size), 1) >= overlap) | (index == 0)
            g_hi, g_lo = split(gain[pl.ds(k, size)].reshape(1, size))
            which = jnp.where(fresh, fob[pl.ds(k, size)].reshape(1, size) - starts[piece], -1)
            which = which.astype(F32).astype(BF16)
            hits = [columns(wide) == spread(which, j, wide) for j in range(0, size, 128)]
            stack = []
            for value in (g_hi, g_lo):
                row = [
                    jnp.where(hits[j // 128], spread(value, j, wide), nothing)
                    for j in range(0, size, 128)
                ]
                stack.append(jnp.concatenate(row, axis=1))
            if piece == 0:
                b_hi, b_lo = split(jnp.where(fresh, base[pl.ds(k, size)].reshape(1, size), 0.0))
                stack.append(
                    jnp.concatenate(
                        [b_hi.astype(F32), b_lo.astype(F32), jnp.zeros((14, size), F32)], axis=0
                    ).astype(BF16)
                )
                for i, (start, length) in enumerate(blocks):
                    pl.when(index == i)(loads[len(first) + i].wait)
            return dot(jnp.concatenate(stack, axis=0), ptdf[:, pl.ds(k, size)], NT)

        def step(i, carry):
            totals[0:height] += product(pl.multiple_of(i * stride, 128), BLOCK, i)
            return carry

        totals[0:height] = jnp.zeros((height, lines), F32)
        lax.fori_loop(0, full, step, 0)
        acc = totals[0:height]
        by_line = jnp.transpose(acc[0:wide] + acc[wide : 2 * wide])
        m_all[:, :, lanes(piece)] = by_line.reshape(nz, lines // nz, wide)
        if piece == 0:
            total_row = acc[2 * wide : 2 * wide + 1] + acc[2 * wide + 1 : 2 * wide + 2]
            base_row[0] = total_row[:, 0 : lines // 2]
            base_row[1] = total_row[:, lines // 2 :]

    def piece_of(piece, long_sign, start, land):
        sides = (
            (long_sign, LONG, half, 0 if long_sign > 0 else 1),
            (-long_sign, SHORT, half - 1, 0 if long_sign < 0 else 1),
        )
        return piece, sides, start, land

    pieces = [
        piece_of(
            p,
            1 if p == 0 else -1,
            lambda d, p=p: m_all.at[d, :, lanes(p)],
            lambda way, k, p=p: ring.at[way, k, :, lanes(p)],
        )
        for p in range(PIECES)
    ]
    pieces.append(
        piece_of(
            PIECES, -1, lambda d: base_row.at[d // (nz // 2)], lambda way, k: base_in.at[way, k]
        )
    )

    def toward(sign, k):
        return lax.rem(z + sign * k + nz, nz)

    def hop(piece, side, k, source):
        index, _, _, land = piece
        sign, stops, _, way = side
        return pltpu.make_async_remote_copy(
            src_ref=source,
            dst_ref=land(way, k),
            send_sem=ring_s.at[index, way, k],
            recv_sem=ring_r.at[index, way, k],
            device_id={"bus": toward(sign, k - next_stop(stops, k))},
            device_id_type=MESH,
        )

    def arrived(piece, side, k):
        hop(piece, side, k, piece[3](side[3], k)).wait_recv()

    sent = []

    def direct(piece, level):
        _, sides, start, _ = piece
        for k in range(half, 0, -1):
            for side in sides:
                sign, stops, far, _ = side
                if k <= far and k not in stops and next_stop(stops, k) == stops[level]:
                    copy = hop(piece, side, k, start(toward(sign, k)))
                    copy.start()
                    sent.append(copy)

    def merge(piece, level):
        _, sides, start, land = piece
        for side in sides:
            sign, stops, far, way = side
            c = stops[level]
            members = [k for k in range(far, 0, -1) if next_stop(stops, k) == c]
            block = start(toward(sign, c))[...]
            for k in members:
                arrived(piece, side, k)
                block = block + land(way, k)[...]
            land(way, members[0])[...] = block
            copy = hop(piece, side, c, land(way, members[0]))
            copy.start()
            sent.append(copy)

    def collect(piece):
        _, sides, start, land = piece
        block = start(z)[...]
        for side in sides:
            for k in range(side[2], 0, -1):
                if next_stop(side[1], k) == 0:
                    arrived(piece, side, k)
                    block = block + land(side[3], k)[...]
        return block

    def prepare():
        for copy in loads[len(first) + len(blocks) :]:
            copy.wait()
        point = lax.broadcasted_iota(jnp.int32, (POINTS, factors), 0)
        digits = jnp.zeros((POINTS, factors), jnp.int32)
        for bit in range(7):
            picked = lax.shift_right_logical(point, bit) & 1
            digits = digits ^ (picked * dirs[bit : bit + 1, :])
        table[...] = digits
        hi, lo = split(chol[...])
        c_hi[...] = hi
        c_lo[...] = lo

    def shadow(t, carry):
        rows = pl.ds(pl.multiple_of(t * POINTS, POINTS), POINTS)
        normal = draw(table[...] ^ shifts[pl.ds(t, 1), :])
        hi, lo = split(normal)
        n_hi[rows, :] = hi
        n_lo[rows, :] = lo
        m_hi, m_lo = split(mean[...].reshape(1, factors))
        both = jnp.concatenate(
            [m_hi.astype(F32), m_lo.astype(F32), jnp.zeros((14, factors), F32)], axis=0
        ).astype(BF16)
        first = dot(both, hi, NT)
        second = dot(both, lo, NT)
        lik[pl.ds(t, 1), :] = jnp.exp(-(first[0:1, :] + (first[1:2, :] + second[0:1, :])))
        return carry

    for copy in loads[: len(first)]:
        copy.wait()
    gather(0)
    pl.semaphore_wait(barrier, 2 * reach + nl // 2)
    direct(pieces[0], 0)
    direct(pieces[PIECES], 0)
    direct(pieces[0], 1)
    gather(1)
    direct(pieces[1], 0)
    direct(pieces[1], 1)
    direct(pieces[PIECES], 1)
    prepare()
    for level in range(len(LONG)):
        lax.fori_loop(GAPS[level][0], GAPS[level][1], shadow, 0)
        if level < len(LONG) - 1:
            for piece in pieces:
                merge(piece, level)
        if level == 0:
            for piece in pieces:
                direct(piece, 2)

    own_lines = lines // nz
    base_line = collect(pieces[PIECES])
    base_line = jnp.concatenate([base_line, base_line], axis=1)
    mine = lax.broadcasted_iota(jnp.int32, (own_lines, lines), 1) == (
        lax.broadcasted_iota(jnp.int32, (own_lines, lines), 0) + z * own_lines
    )
    base_col = jnp.sum(jnp.where(mine, base_line, 0.0), axis=1, keepdims=True)
    rate_col = jnp.sum(jnp.where(mine, rating[...].reshape(1, lines).astype(F32) * 0.01, 0.0), axis=1, keepdims=True)
    steep = SHARP / rate_col

    total_m = jnp.concatenate([collect(pieces[p]) for p in range(PIECES)], axis=1)

    h, l = split(total_m)
    g = dot(h, c_hi[...], NN) + (dot(l, c_hi[...], NN) + dot(h, c_lo[...], NN))
    const = jnp.sum(g * mean[...].reshape(1, factors), axis=1, keepdims=True) + base_col
    gh, gl = split(g)
    both = jnp.concatenate([gh.astype(F32), gl.astype(F32)], axis=0).astype(BF16)
    low_lane = lax.broadcasted_iota(jnp.int32, (8, POINTS), 1) < POINTS // 2
    for k in range(8):
        rows = pl.ds(k * POINTS, POINTS)
        first = dot(both, n_hi[rows, :], NT)
        second = dot(gh, n_lo[rows, :], NT)
        x = first[0:own_lines, :] + (first[own_lines:, :] + second) + const
        v = jnp.abs(x) * steep - SHARP
        soft = jnp.maximum(v, 0.0) + jnp.log1p(jnp.exp(-jnp.abs(v)))
        share[k : k + 1, :] = jnp.sum(soft, axis=0, keepdims=True) * (1.0 / (SHARP * lines * nl))
        top, low = x[0:8, :], x[8:16, :]
        send[2 * k] = jnp.where(low_lane, top, pltpu.roll(low, POINTS // 2, 1))
        send[2 * k + 1] = jnp.where(low_lane, pltpu.roll(top, POINTS // 2, 1), low)

    def send_to(source, slots, slot, send_sem, recv_sem, axis, peer):
        return pltpu.make_async_remote_copy(
            src_ref=source,
            dst_ref=slots.at[slot],
            send_sem=send_sem,
            recv_sem=recv_sem,
            device_id={axis: peer},
            device_id_type=MESH,
        )

    partner = pltpu.make_async_remote_copy(
        src_ref=share,
        dst_ref=pair_in,
        send_sem=cs,
        recv_sem=cr,
        device_id={"line": chip * 2 + 1 - core},
        device_id_type=MESH,
    )
    partner.start()
    recv[z] = send[z]
    partner.wait_recv()
    chip_sum[...] = share[...] + pair_in[...]

    def plane_copy(n, slot):
        peer = chip_at(*plane_order[n])
        slot = chip if slot is None else peer
        return send_to(chip_sum, plane_in, slot, ls.at[n], lr.at[slot], "line", peer * 2 + core)

    def flow_copy(d, slot):
        peer = lax.rem(z + d, nz)
        slot = z if slot is None else peer
        return send_to(send.at[peer], recv, slot, fs.at[d], fr.at[slot], "bus", peer)

    def deep_copy(d, slot):
        peer = lax.rem(z + d, nz)
        slot = z if slot is None else peer
        return send_to(plane_sum, deep_in, slot, ds.at[d], dr.at[slot], "bus", peer)

    for n in range(len(plane_order)):
        copy = plane_copy(n, None)
        copy.start()
        sent.append(copy)
    for d in z_order:
        copy = flow_copy(d, None)
        copy.start()
        sent.append(copy)
    plane_in[chip] = chip_sum[...]
    for n in range(len(plane_order)):
        plane_copy(n, n).wait_recv()
    partial = plane_in[0]
    for j in range(1, nl // 2):
        partial = partial + plane_in[j]
    plane_sum[...] = partial
    for d in z_order:
        copy = deep_copy(d, None)
        copy.start()
        sent.append(copy)
    deep_in[z] = partial

    for d in z_order:
        flow_copy(d, d).wait_recv()
    tiles = []
    for j in range(nz):
        tile = recv[j]
        tiles.append(tile)
        tiles.append(pltpu.roll(tile, POINTS // 2, 1))
    by_line = jnp.concatenate(tiles, axis=0)
    flows_o[...] = jnp.transpose(by_line)[0 : POINTS // 2, :]

    for d in z_order:
        deep_copy(d, d).wait_recv()
    total_over = deep_in[0]
    for j in range(1, nz):
        total_over = total_over + deep_in[j]
    over[...] = total_over
    emphasis = lik[...] * total_over
    total = jnp.sum(jnp.sum(emphasis, axis=1, keepdims=True), axis=0, keepdims=True)
    inverse = 1.0 / total
    flat = jnp.concatenate([emphasis[k : k + 1, :] for k in range(8)], axis=1)
    e_hi, e_lo = split(flat)
    both = jnp.concatenate(
        [e_hi.astype(F32), e_lo.astype(F32), jnp.zeros((14, flat.shape[1]), F32)], axis=0
    ).astype(BF16)
    first = dot(both, n_hi[...], NN)
    second = dot(both, n_lo[...], NN)
    moved = first[0:1, :] + (first[1:2, :] + second[0:1, :])
    newmean_o[...] = mean[...].reshape(1, factors) + moved * inverse
    row = over[pl.ds(z // 2, 1), :]
    like_row = lik[pl.ds(z // 2, 1), :]
    odd = lax.rem(z, 2) == 1
    row = jnp.where(odd, row[:, POINTS // 2 :], row[:, 0 : POINTS // 2])
    like_row = jnp.where(odd, like_row[:, POINTS // 2 :], like_row[:, 0 : POINTS // 2])
    overload_o[...] = row
    weight_o[...] = (float(8 * POINTS) * like_row) * row * inverse

    partner.wait_send()
    for copy in sent:
        copy.wait_send()


def deliver(*refs):
    sources, targets, sem = refs[0:4], refs[4:8], refs[8]
    copies = []
    for i, (source, target) in enumerate(zip(sources, targets)):
        if len(target.shape) == 1:
            source = source.at[0]
        copies.append(pltpu.make_async_copy(source, target, sem.at[i]))
    for copy in copies:
        copy.start()
    for copy in copies:
        copy.wait()


def per_device(nz, nl, ptdf, base, gain, fob, rating, dirs, shifts, chol, mean):
    lines, buses = ptdf.shape
    factors = chol.shape[0]
    half = nz // 2
    own = lines // nz
    scen = shifts.shape[0] * POINTS
    vm, dma = pltpu.VMEM, pltpu.SemaphoreType.DMA
    anywhere = pl.BlockSpec(memory_space=pl.ANY)
    inside = pl.BlockSpec(memory_space=pltpu.VMEM)
    n_loads = 8 + -(-buses // BLOCK)
    flows, overload, weight, new_mean = pl.pallas_call(
        functools.partial(kernel, nz, nl),
        out_shape=(
            jax.ShapeDtypeStruct((scen // nz, lines), F32),
            jax.ShapeDtypeStruct((1, scen // nz), F32),
            jax.ShapeDtypeStruct((1, scen // nz), F32),
            jax.ShapeDtypeStruct((1, factors), F32),
        ),
        in_specs=[anywhere] * 9,
        out_specs=(inside,) * 4,
        scratch_shapes=[
            vm((lines, buses), BF16),
            vm((buses,), F32),
            vm((buses,), F32),
            vm((buses,), jnp.int32),
            vm((lines,), jnp.int32),
            vm(dirs.shape, jnp.int32),
            vm(shifts.shape, jnp.int32),
            vm(chol.shape, F32),
            vm((factors,), F32),
            vm((nz, own, factors), F32),
            vm((2 * max(WIDTHS) + 16, lines), F32),
            vm((2, half + 1, own, factors), F32),
            vm((POINTS, factors), jnp.int32),
            vm((scen, factors), BF16),
            vm((scen, factors), BF16),
            vm(chol.shape, BF16),
            vm(chol.shape, BF16),
            vm((8, POINTS), F32),
            vm((2, 1, POINTS), F32),
            vm((2, half + 1, 1, POINTS), F32),
            vm((nz, 8, POINTS), F32),
            vm((nz, 8, POINTS), F32),
            vm((8, POINTS), F32),
            vm((8, POINTS), F32),
            vm((8, POINTS), F32),
            vm((nl // 2, 8, POINTS), F32),
            vm((8, POINTS), F32),
            vm((nz, 8, POINTS), F32),
            vm((8, POINTS), F32),
            dma((n_loads,)),
            dma((PIECES + 1, 2, half + 1)),
            dma((PIECES + 1, 2, half + 1)),
            dma((nz,)),
            dma((nz,)),
            dma(()),
            dma(()),
            dma((nl // 2,)),
            dma((nl // 2,)),
            dma((nz,)),
            dma((nz,)),
        ],
        compiler_params=pltpu.CompilerParams(
            collective_id=0, has_side_effects=True, vmem_limit_bytes=40 * 1024 * 1024
        ),
    )(
        *[
            pltpu.with_memory_space_constraint(a, pltpu.HBM)
            for a in (ptdf, base, gain, fob, rating, dirs, shifts, chol, mean)
        ]
    )
    results = (flows, overload, weight, new_mean)
    return pl.pallas_call(
        deliver,
        out_shape=tuple(jax.ShapeDtypeStruct(a.shape if a.shape[0] > 1 else a.shape[1:], F32) for a in results),
        in_specs=[pl.BlockSpec(memory_space=pltpu.VMEM)] * 4,
        out_specs=(anywhere,) * 4,
        scratch_shapes=[dma((4,))],
        compiler_params=pltpu.CompilerParams(vmem_limit_bytes=1024 * 1024),
    )(*results)


def solution(mesh):
    nz, nl = mesh.shape["bus"], mesh.shape["line"]
    return jax.shard_map(
        functools.partial(per_device, nz, nl),
        mesh=mesh,
        in_specs=(P("line", "bus"), P("bus"), P("bus"), P("bus"), P("line"), P(), P(), P(), P()),
        out_specs=(P("bus", "line"), P("bus"), P("bus"), P()),
        check_vma=False,
    )
```
